256 devices in a mesh: rows: 32 (over z, x), cols: 8 (over y, core).
Axes of the slice: x: 4, y: 4, z: 8, core: 2. Of those that a mesh axis runs over, the one named last changes fastest.
Arguments:
- block_values: bfloat16 [256, 256, 128, 128], P('rows', 'cols')
- block_columns: int32 [256, 256], P('rows', 'cols'), may hold values from 0 to 1023, as said below
- row_counts: int32 [256, 8], P('rows', 'cols'), may hold values from 1 to 32, as said below
- sketch: bfloat16 [1048576, 256], P(('rows', 'cols')), may hold values from -6 to 6
Outputs:
- basis: float32 [32768, 256], P(('rows', 'cols'))
- triangle: float32 [256, 256], replicated
The draws below stay inside these ranges and needn't reach their ends.
Inputs may be any that keep to these rules, and one draw needn't show every extreme that they name: row_counts[b, c] counts the live slots among slots c * 32 to c * 32 + 31 of block-row b; some entry equals 32. `block_columns`: take the 8 x 32 slots of one index of rows and one column group c; among them at most 12 name block-columns j with the same j // 32, and in every such set some j // 32 is named by exactly 12 slots.
All inputs are finite; a program needn't handle non-finite values.
Results may differ from the reference program's by a relative error of at most 0.0003.
Values may be sent and summed in bfloat16 or wider, within the bound.
No kernel may reach another device: no remote copies, remote signals or barrier semaphores. Data moves between devices by JAX's collectives and lax.ppermute only.
A program may use at most 128 MiB of HBM per device.

```python
import jax
import jax.numpy as jnp
from jax import lax

BR_DEV = 8
S = 32
BS = 128
K = 256
NB = 256
SLOTS_ROW = 256
LB = 1024
BPD = 32
CAP = 12
N = 1048576
N_ROWS = 32
N_COLS = 8


def draw_block_values(key, part):
    first_key = jax.random.fold_in(key, 0)
    shape = (NB, SLOTS_ROW, BS, BS)
    fan_width = BS * SLOTS_ROW / 2.0
    normal_part = jax.random.normal(first_key, shape, jnp.float32)
    steps_along = jnp.arange(NB, dtype=jnp.float32) / max(NB - 1, 1)
    row_scale = jnp.exp(0.5 * 1.0986123 * steps_along)
    return (normal_part * row_scale[:, None, None, None] / jnp.sqrt(fan_width)).astype(jnp.bfloat16)


def draw_row_counts(key, part):
    first_key, second_key = jax.random.split(key)
    group_count = SLOTS_ROW // S
    counts = jax.random.randint(first_key, (NB, group_count), 1, S + 1)
    where_full = jax.random.randint(second_key, (), 0, NB * group_count)
    flat_ids = jnp.arange(NB * group_count, dtype=jnp.int32).reshape(NB, group_count)
    return jnp.where(flat_ids == where_full, S, counts).astype(jnp.int32)


def device_columns(device_key):
    first_key, second_key, third_key, fourth_key = jax.random.split(device_key, 4)
    slot_total = BR_DEV * S
    pool_size = N_ROWS * CAP
    busiest = jax.random.randint(first_key, (), 0, N_ROWS)
    pool_owners = jnp.arange(pool_size, dtype=jnp.int32) // CAP
    scores = jax.random.permutation(second_key, pool_size).astype(jnp.int32)
    scores = jnp.where(pool_owners == busiest, scores - pool_size, scores)
    ordering = jnp.argsort(scores)
    chosen = pool_owners[ordering][:slot_total]
    chosen = jax.random.permutation(third_key, chosen)
    within = jax.random.randint(fourth_key, (slot_total,), 0, BPD)
    return (chosen * BPD + within).astype(jnp.int32)


def draw_block_columns(key, part):
    device_keys = jax.random.split(jax.random.fold_in(key, 17), N_ROWS * N_COLS)
    columns_all = jax.vmap(device_columns)(device_keys)
    columns_all = columns_all.reshape(N_ROWS, N_COLS, BR_DEV, S).transpose(0, 2, 1, 3)
    return columns_all.reshape(NB, SLOTS_ROW).astype(jnp.int32)


def levels(key, shape, cuts, least, top_value):
    factor_of = 1.0
    for axis_at, shards_of in cuts:
        heights = jax.random.uniform(jax.random.fold_in(jax.random.fold_in(key, 6), axis_at), (shards_of,), jnp.float32, least / len(cuts), top_value / len(cuts))
        factor_of = factor_of * jnp.repeat(jnp.exp(heights), shape[axis_at] // shards_of).reshape((-1,) + (1,) * (len(shape) - 1 - axis_at))
    return factor_of


def centred(key, extent, deviation, most, cuts=(), kind=jnp.bfloat16):
    drawn = jax.random.normal(key, extent, jnp.float32) * deviation
    if len(cuts) > 0:
        drawn = levels(key, extent, cuts, -0.22, 0.18) * drawn
    return jnp.clip(drawn, min=-most, max=most).astype(kind)


def setup_inputs(seed: int = 0) -> dict:
    splits = jax.random.split(jax.random.key(seed), 5)
    return {
        "block_values": draw_block_values(jax.random.fold_in(splits[4], 71), 0),
        "block_columns": draw_block_columns(jax.random.fold_in(splits[4], 71), 0),
        "row_counts": draw_row_counts(jax.random.fold_in(splits[4], 71), 0),
        "sketch": centred(splits[3], (N, K), 1.0, 6.0, ((0, 256),)),
    }


def reference(block_values, block_columns, row_counts, sketch):
    group_count = N_COLS
    groups = sketch.reshape(N_ROWS, group_count, BPD * BS, K).transpose(1, 0, 2, 3)
    groups = groups.reshape(group_count, LB, BS, K)
    group_ids = jnp.arange(group_count, dtype=jnp.int32)[:, None]
    slot_ids = jnp.arange(S, dtype=jnp.int32)[None, :]

    def one_row(entries):
        values_row, columns_row, counts_row = entries
        picked = groups[group_ids, columns_row.reshape(group_count, S)]
        live_mask = (slot_ids < counts_row[:, None]).astype(jnp.float32)
        picked = picked.astype(jnp.float32) * live_mask[:, :, None, None]
        values_row = values_row.reshape(group_count, S, BS, BS).astype(jnp.float32)
        return jnp.einsum('csab,csbk->ak', values_row, picked)
    image_all = lax.map(one_row, (block_values, block_columns, row_counts)).reshape(NB * BS, K)
    gram_matrix = jnp.dot(image_all.T.astype(jnp.float32), image_all.astype(jnp.float32), precision=lax.Precision.HIGHEST, preferred_element_type=jnp.float32) / (NB * BS)
    lower_factor = jnp.linalg.cholesky(gram_matrix)
    basis_rows = jax.scipy.linalg.solve_triangular(lower_factor, image_all.T, lower=True).T
    return (basis_rows, lower_factor.T)
```

```python
import functools

import jax
import jax.numpy as jnp
from jax import lax
from jax.experimental import pallas as pl
from jax.experimental.pallas import tpu as pltpu
from jax.sharding import Mesh
from jax.sharding import PartitionSpec as P

NZ, NX, NY, NC = 8, 4, 4, 2
CAP = 12
BR, S, BS, K = 8, 32, 128, 256
BPD = 32
ENTRIES = NX * CAP
ROWS = NX * BR
HIGH = lax.Precision.HIGHEST


def ring(n, shift):
    return [(i, (i + shift) % n) for i in range(n)]


def products_kernel(ds, halves, first, last, *refs):
    refs = list(refs)
    tbl, num = refs[0], refs[1]
    vals = refs[2:6]
    pos = 6
    tabs = []
    for h in halves:
        tabs.append(refs[pos : pos + h])
        pos += h
    if not first:
        prev = refs[pos]
        pos += 1
    nouts = 2 if last else 1
    outs = refs[pos : pos + nouts]
    vb, tb, acc, vsem, tsem, psem = refs[pos + nouts :]
    waits = []
    for i, d in enumerate(ds):
        mine = []
        for dx in range(NX):
            mine.append(
                pltpu.make_async_copy(
                    vals[dx].at[d], vb.at[i, pl.ds(dx * CAP, CAP)], vsem.at[i, dx]
                )
            )
        size = BPD // halves[i]
        for h in range(halves[i]):
            mine.append(
                pltpu.make_async_copy(
                    tabs[i][h], tb.at[i, pl.ds(h * size, size)], tsem.at[i, h]
                )
            )
        for c in mine:
            c.start()
        waits.append(mine)
    if first:
        acc[...] = jnp.zeros_like(acc)
    else:
        load = pltpu.make_async_copy(prev, acc.at[pl.ds(0, ROWS)], psem.at[0])
        load.start()
        load.wait()
    for i, d in enumerate(ds):
        for c in waits[i]:
            c.wait()

        def step(j, carry, i=i, d=d):
            for u in range(4):
                entry = tbl[d * ENTRIES + j * 4 + u]
                v = jnp.bitwise_and(entry, 63)
                t = jnp.bitwise_and(lax.shift_right_logical(entry, 6), 31)
                row = lax.shift_right_logical(entry, 11)
                acc[row] += jnp.dot(
                    vb[i, v], tb[i, t], preferred_element_type=jnp.float32
                )
            return carry

        lax.fori_loop(0, (num[d] + 3) // 4, step, 0)
    size = ROWS // nouts
    stores = [
        pltpu.make_async_copy(acc.at[pl.ds(o * size, size)], outs[o], psem.at[o])
        for o in range(nouts)
    ]
    for c in stores:
        c.start()
    for c in stores:
        c.wait()


def products(ds, tbl, num, vals, tabs, prev, last):
    halves = tuple(len(t) for t in tabs)
    first = prev is None
    args = list(vals) + [a for t in tabs for a in t] + ([] if first else [prev])
    shape = (ROWS // 2 if last else ROWS, BS, K)
    out = [jax.ShapeDtypeStruct(shape, jnp.float32)] * (2 if last else 1)
    anyspec = pl.BlockSpec(memory_space=pl.ANY)
    nd = len(ds)
    return pl.pallas_call(
        functools.partial(products_kernel, ds, halves, first, last),
        out_shape=out,
        grid_spec=pltpu.PrefetchScalarGridSpec(
            num_scalar_prefetch=2,
            grid=(1,),
            in_specs=[anyspec] * len(args),
            out_specs=[anyspec] * len(out),
            scratch_shapes=[
                pltpu.VMEM((nd, ENTRIES, BS, BS), jnp.bfloat16),
                pltpu.VMEM((nd, BPD, BS, K), jnp.bfloat16),
                pltpu.VMEM((ROWS + 1, BS, K), jnp.float32),
                pltpu.SemaphoreType.DMA((nd, NX)),
                pltpu.SemaphoreType.DMA((nd, 2)),
                pltpu.SemaphoreType.DMA((2,)),
            ],
        ),
        compiler_params=pltpu.CompilerParams(vmem_limit_bytes=40 << 20),
        cost_estimate=pl.CostEstimate(
            flops=nd * 20 * 2 * BS * BS * K,
            bytes_accessed=nd * (ENTRIES * BS * BS * 2 + BPD * BS * K * 2) + 2 * ROWS * BS * K * 4,
            transcendentals=0,
        ),
        name="products" + "".join(str(d) for d in ds),
    )(tbl, num, *args)


HB = 64


def factor_block(d):
    groups = [d[8 * g : 8 * g + 8, :] for g in range(8)]
    sub = lax.broadcasted_iota(jnp.int32, (8, 128), 0)
    for p in range(8):
        r = groups[p]
        cols = [jnp.broadcast_to(r[:, 8 * p + k : 8 * p + k + 1], (8, 128)) for k in range(8)]
        a = [
            [jnp.broadcast_to(cols[k][i : i + 1, :], (8, 128)) if i <= k else None for k in range(8)]
            for i in range(8)
        ]
        rs = [None] * 8
        rows = []
        for i in range(8):
            piv = a[i][i]
            y = lax.rsqrt(piv)
            rs[i] = y * (1.5 - 0.5 * (piv * y) * y)
            for k in range(i + 1, 8):
                a[i][k] = a[i][k] * rs[i]
            for k in range(i + 1, 8):
                for l in range(k, 8):
                    a[k][l] = a[k][l] - a[i][k] * a[i][l]
            row = jnp.broadcast_to(r[i : i + 1, :], (8, 128))
            for k in range(i):
                row = row - a[k][i] * rows[k]
            rows.append(row * rs[i])
        for g in range(p + 1, 8):
            cur = groups[g]
            mult = []
            for i in range(8):
                m = jnp.broadcast_to(cur[:, 8 * p + i : 8 * p + i + 1], (8, 128))
                for k in range(i):
                    m = m - mult[k] * a[k][i]
                mult.append(m * rs[i])
            for i in range(8):
                cur = cur - mult[i] * rows[i]
            groups[g] = cur
        new = rows[0]
        for i in range(1, 8):
            new = jnp.where(sub == i, rows[i], new)
        groups[p] = new
    return jnp.concatenate(groups, axis=0)


def factor_kernel(g_ref, xt_ref, tri_ref, basis_ref, a_ref, w_ref):
    a_ref[...] = g_ref[...]
    w_ref[...] = xt_ref[...]
    lane = lax.broadcasted_iota(jnp.int32, (HB, 128), 1)
    srow = lax.broadcasted_iota(jnp.int32, (HB, 128), 0)
    eye = jnp.where(lane - HB == srow, 1.0, 0.0).astype(jnp.float32)
    low = lane < HB
    rown = lax.broadcasted_iota(jnp.int32, (HB, K), 0)
    coln = lax.broadcasted_iota(jnp.int32, (HB, K), 1)
    for b in range(K // HB):
        lo, hi = b * HB, (b + 1) * HB
        tile = a_ref[lo:hi, 128 * (b // 2) : 128 * (b // 2) + 128]
        if b % 2:
            tile = pltpu.roll(tile, HB, 1)
        res = factor_block(jnp.where(low, tile, eye))
        inv = jnp.where(low, 0.0, res)
        zero = jnp.zeros((HB, K + BS), jnp.float32)
        both = jnp.concatenate([a_ref[lo:hi, :], w_ref[lo:hi, :]], axis=1)
        out = jnp.dot(
            inv,
            jnp.concatenate([zero, both], axis=0),
            precision=HIGH,
            preferred_element_type=jnp.float32,
        )
        upper = jnp.where(coln >= rown + lo, out[:, :K], 0.0)
        tri_ref[lo:hi, :] = upper
        w_ref[lo:hi, :] = out[:, K:]
        if hi < K:
            new = jnp.concatenate([upper, out[:, K:]], axis=1)
            upd = lax.dot_general(
                upper,
                new,
                (((0,), (0,)), ((), ())),
                precision=HIGH,
                preferred_element_type=jnp.float32,
            )
            a_ref[hi:, :] = a_ref[hi:, :] - upd[hi:, :K]
            w_ref[hi:, :] = w_ref[hi:, :] - upd[hi:, K:]
    basis_ref[...] = w_ref[...].T


def factor(gram, xt):
    vm = pl.BlockSpec(memory_space=pltpu.VMEM)
    return pl.pallas_call(
        factor_kernel,
        out_shape=[
            jax.ShapeDtypeStruct((K, K), jnp.float32),
            jax.ShapeDtypeStruct((BS, K), jnp.float32),
        ],
        in_specs=[vm, vm],
        out_specs=[vm, vm],
        scratch_shapes=[pltpu.VMEM((K, K), jnp.float32), pltpu.VMEM((K, BS), jnp.float32)],
        name="factor",
    )(gram, xt)


def rank_in_owner(owner):
    n = owner.shape[-1]
    earlier = jnp.arange(n)[None, :] < jnp.arange(n)[:, None]
    same = owner[..., None, :] == owner[..., :, None]
    return jnp.sum((same & earlier).astype(jnp.int32), axis=-1)


def per_device(block_values, block_columns, row_counts, sketch):
    z, x, core = lax.axis_index("z"), lax.axis_index("x"), lax.axis_index("core")
    blocks = sketch.reshape(2, BPD // 2, BS, K)
    have = {0: [sketch.reshape(BPD, BS, K)]}
    fwd = {0: [blocks[0], blocks[1]]}
    bwd = {0: [blocks[0], blocks[1]]}
    for step in range(1, 5):
        fwd[step] = [None, None]
        bwd[step] = [None, None]
        for h in range(2):
            if step < 4 or h == 0:
                fwd[step][h] = lax.ppermute(fwd[step - 1][h], "z", ring(NZ, 1))
            if step < 4 or h == 1:
                bwd[step][h] = lax.ppermute(bwd[step - 1][h], "z", ring(NZ, -1))
        if step < 4:
            have[NZ - step] = fwd[step]
            have[step] = bwd[step]
        else:
            have[4] = [fwd[4][0], bwd[4][1]]

    slots = BR * S
    live = jnp.arange(S, dtype=jnp.int32)[None, :] < row_counts
    meta = jnp.where(live, block_columns, -1).reshape(slots)
    ids = jnp.arange(slots, dtype=jnp.int32)
    own = meta // BPD
    dist_z = (own // NX - z) % NZ
    dist_x = (own % NX - x) % NX
    owner = jnp.where(meta < 0, NX * NZ, dist_x * NZ + dist_z)
    place = owner * CAP + rank_in_owner(owner)
    spots = jnp.arange(NX * NZ * CAP, dtype=jnp.int32)
    wanted = jnp.sum(jnp.where(place[:, None] == spots[None, :], ids[:, None], 0), axis=0)
    flat_values = block_values.reshape(slots, BS, BS)
    vals = []
    metas = []
    for dx in range(NX):
        part = wanted[dx * NZ * CAP : (dx + 1) * NZ * CAP]
        sent = flat_values.at[part].get(mode="promise_in_bounds")
        if dx:
            sent = lax.ppermute(sent, "x", ring(NX, dx))
            metas.append(lax.ppermute(meta.reshape(2, 128), "x", ring(NX, dx)).reshape(slots))
        else:
            metas.append(meta)
        vals.append(sent.reshape(NZ, CAP, BS, BS))

    got = jnp.stack(metas)
    own = got // BPD
    match = (got >= 0) & (own % NX == x)
    dist = jnp.where(match, (own // NX - z) % NZ, NZ)
    rank = rank_in_owner(dist)
    hits = (dist[:, :, None] == jnp.arange(NZ)[None, None, :]).astype(jnp.int32)
    counts = jnp.sum(hits, axis=1)
    offsets = jnp.cumsum(counts, axis=0) - counts
    number = jnp.sum(counts, axis=0)
    shift = jnp.arange(NX, dtype=jnp.int32)[:, None]
    source = (x - shift) % NX
    entry = jnp.sum(hits * offsets[:, None, :], axis=2) + rank
    where = jnp.where(match, dist * ENTRIES + entry, -1).reshape(-1)
    block_row = (ids // S)[None, :]
    row = ((block_row % NC) ^ core) * (ROWS // 2) + source * NY + block_row // NC
    packed = shift * CAP + rank + 64 * (got % BPD) + 2048 * row
    dummy = 2048 * ROWS
    spots = jnp.arange(NZ * ENTRIES, dtype=jnp.int32)
    table = dummy + jnp.sum(
        jnp.where(where[:, None] == spots[None, :], packed.reshape(-1)[:, None] - dummy, 0), axis=0
    )

    prev = None
    groups = [(0, 1, 7, 2, 6), (3, 5), (4,)]
    for n, ds in enumerate(groups):
        last = n == len(groups) - 1
        prev = products(ds, table, number, vals, [have[d] for d in ds], prev, last)
        if not last:
            prev = prev[0]
    mine, other = prev
    half = mine + lax.ppermute(other, "core", ring(NC, 1))
    image = jnp.sum(lax.all_to_all(half, ("x", "y"), 0, 0, tiled=True), axis=0)

    gram = lax.dot_general(
        image, image, (((0,), (0,)), ((), ())), precision=HIGH, preferred_element_type=jnp.float32
    )
    plane = ("x", "y", "core")
    n_plane = NX * NY * NC
    piece = K // n_plane
    gram = gram.reshape(n_plane, piece, K)
    part = jnp.sum(lax.all_to_all(gram, plane, 0, 0, tiled=True), axis=0)
    part = jnp.broadcast_to(part[None], (NZ, piece, K))
    part = jnp.sum(lax.all_to_all(part, "z", 0, 0, tiled=True), axis=0) / (NZ * n_plane * BS)
    part = jnp.broadcast_to(part[None], (n_plane, piece, K))
    gram = lax.all_to_all(part, plane, 0, 0, tiled=True).reshape(K, K)
    triangle, basis = factor(gram, image.T)
    return basis, triangle


def solution(mesh):
    axes = ("z", "x", "y", "core")
    fine = Mesh(mesh.devices.reshape(NZ, NX, NY, NC), axes)
    rows, cols = ("z", "x"), ("y", "core")
    return jax.shard_map(
        per_device,
        mesh=fine,
        in_specs=(P(rows, cols, None, None), P(rows, cols), P(rows, cols), P(axes, None)),
        out_specs=(P(axes, None), P()),
        check_vma=False,
    )
```

```python
import functools

import jax
import jax.numpy as jnp
from jax import lax
from jax.experimental import pallas as pl
from jax.experimental.pallas import tpu as pltpu
from jax.sharding import Mesh
from jax.sharding import PartitionSpec as P

NZ, NX, NY, NC = 8, 4, 4, 2
CAP = 12
BR, S, BS, K = 8, 32, 128, 256
BPD = 32
ENTRIES = NX * CAP
ROWS = NX * BR
HIGH = lax.Precision.HIGHEST


def ring(n, shift):
    return [(i, (i + shift) % n) for i in range(n)]


def products_kernel(ds, halves, first, last, *refs):
    refs = list(refs)
    tbl, num = refs[0], refs[1]
    vals = refs[2:6]
    pos = 6
    tabs = []
    for h in halves:
        tabs.append(refs[pos : pos + h])
        pos += h
    if not first:
        prev = refs[pos]
        pos += 1
    nouts = 2 if last else 1
    outs = refs[pos : pos + nouts]
    vb, tb, acc, vsem, tsem, psem = refs[pos + nouts :]
    waits = []
    for i, d in enumerate(ds):
        mine = []
        for dx in range(NX):
            mine.append(
                pltpu.make_async_copy(
                    vals[dx].at[d], vb.at[i, pl.ds(dx * CAP, CAP)], vsem.at[i, dx]
                )
            )
        size = BPD // halves[i]
        for h in range(halves[i]):
            mine.append(
                pltpu.make_async_copy(
                    tabs[i][h], tb.at[i, pl.ds(h * size, size)], tsem.at[i, h]
                )
            )
        for c in mine:
            c.start()
        waits.append(mine)
    if first:
        acc[...] = jnp.zeros_like(acc)
    else:
        load = pltpu.make_async_copy(prev, acc.at[pl.ds(0, ROWS)], psem.at[0])
        load.start()
        load.wait()
    for i, d in enumerate(ds):
        for c in waits[i]:
            c.wait()

        def step(j, carry, i=i, d=d):
            for u in range(4):
                entry = tbl[d * ENTRIES + j * 4 + u]
                v = jnp.bitwise_and(entry, 63)
                t = jnp.bitwise_and(lax.shift_right_logical(entry, 6), 31)
                row = lax.shift_right_logical(entry, 11)
                acc[row] += jnp.dot(
                    vb[i, v], tb[i, t], preferred_element_type=jnp.float32
                )
            return carry

        lax.fori_loop(0, (num[d] + 3) // 4, step, 0)
    size = ROWS // nouts
    stores = [
        pltpu.make_async_copy(acc.at[pl.ds(o * size, size)], outs[o], psem.at[o])
        for o in range(nouts)
    ]
    for c in stores:
        c.start()
    for c in stores:
        c.wait()


def products(ds, tbl, num, vals, tabs, prev, last):
    halves = tuple(len(t) for t in tabs)
    first = prev is None
    args = list(vals) + [a for t in tabs for a in t] + ([] if first else [prev])
    shape = (ROWS // 2 if last else ROWS, BS, K)
    out = [jax.ShapeDtypeStruct(shape, jnp.float32)] * (2 if last else 1)
    anyspec = pl.BlockSpec(memory_space=pl.ANY)
    nd = len(ds)
    return pl.pallas_call(
        functools.partial(products_kernel, ds, halves, first, last),
        out_shape=out,
        grid_spec=pltpu.PrefetchScalarGridSpec(
            num_scalar_prefetch=2,
            grid=(1,),
            in_specs=[anyspec] * len(args),
            out_specs=[anyspec] * len(out),
            scratch_shapes=[
                pltpu.VMEM((nd, ENTRIES, BS, BS), jnp.bfloat16),
                pltpu.VMEM((nd, BPD, BS, K), jnp.bfloat16),
                pltpu.VMEM((ROWS + 1, BS, K), jnp.float32),
                pltpu.SemaphoreType.DMA((nd, NX)),
                pltpu.SemaphoreType.DMA((nd, 2)),
                pltpu.SemaphoreType.DMA((2,)),
            ],
        ),
        compiler_params=pltpu.CompilerParams(vmem_limit_bytes=40 << 20),
        cost_estimate=pl.CostEstimate(
            flops=nd * 20 * 2 * BS * BS * K,
            bytes_accessed=nd * (ENTRIES * BS * BS * 2 + BPD * BS * K * 2) + 2 * ROWS * BS * K * 4,
            transcendentals=0,
        ),
        name="products" + "".join(str(d) for d in ds),
    )(tbl, num, *args)


HB = 64


def factor_block(d):
    groups = [d[8 * g : 8 * g + 8, :] for g in range(8)]
    sub = lax.broadcasted_iota(jnp.int32, (8, 128), 0)
    for p in range(8):
        r = groups[p]
        cols = [jnp.broadcast_to(r[:, 8 * p + k : 8 * p + k + 1], (8, 128)) for k in range(8)]
        a = [
            [jnp.broadcast_to(cols[k][i : i + 1, :], (8, 128)) if i <= k else None for k in range(8)]
            for i in range(8)
        ]
        rs = [None] * 8
        rows = []
        for i in range(8):
            piv = a[i][i]
            y = lax.rsqrt(piv)
            rs[i] = y * (1.5 - 0.5 * (piv * y) * y)
            for k in range(i + 1, 8):
                a[i][k] = a[i][k] * rs[i]
            for k in range(i + 1, 8):
                for l in range(k, 8):
                    a[k][l] = a[k][l] - a[i][k] * a[i][l]
            row = jnp.broadcast_to(r[i : i + 1, :], (8, 128))
            for k in range(i):
                row = row - a[k][i] * rows[k]
            rows.append(row * rs[i])
        for g in range(p + 1, 8):
            cur = groups[g]
            mult = []
            for i in range(8):
                m = jnp.broadcast_to(cur[:, 8 * p + i : 8 * p + i + 1], (8, 128))
                for k in range(i):
                    m = m - mult[k] * a[k][i]
                mult.append(m * rs[i])
            for i in range(8):
                cur = cur - mult[i] * rows[i]
            groups[g] = cur
        new = rows[0]
        for i in range(1, 8):
            new = jnp.where(sub == i, rows[i], new)
        groups[p] = new
    return jnp.concatenate(groups, axis=0)


def factor_kernel(g_ref, xt_ref, tri_ref, basis_ref, a_ref, w_ref):
    a_ref[...] = g_ref[...]
    w_ref[...] = xt_ref[...]
    lane = lax.broadcasted_iota(jnp.int32, (HB, 128), 1)
    srow = lax.broadcasted_iota(jnp.int32, (HB, 128), 0)
    eye = jnp.where(lane - HB == srow, 1.0, 0.0).astype(jnp.float32)
    low = lane < HB
    rown = lax.broadcasted_iota(jnp.int32, (HB, K), 0)
    coln = lax.broadcasted_iota(jnp.int32, (HB, K), 1)
    for b in range(K // HB):
        lo, hi = b * HB, (b + 1) * HB
        tile = a_ref[lo:hi, 128 * (b // 2) : 128 * (b // 2) + 128]
        if b % 2:
            tile = pltpu.roll(tile, HB, 1)
        res = factor_block(jnp.where(low, tile, eye))
        inv = jnp.where(low, 0.0, res)
        zero = jnp.zeros((HB, K + BS), jnp.float32)
        both = jnp.concatenate([a_ref[lo:hi, :], w_ref[lo:hi, :]], axis=1)
        out = jnp.dot(
            inv,
            jnp.concatenate([zero, both], axis=0),
            precision=HIGH,
            preferred_element_type=jnp.float32,
        )
        upper = jnp.where(coln >= rown + lo, out[:, :K], 0.0)
        tri_ref[lo:hi, :] = upper
        w_ref[lo:hi, :] = out[:, K:]
        if hi < K:
            new = jnp.concatenate([upper, out[:, K:]], axis=1)
            upd = lax.dot_general(
                upper,
                new,
                (((0,), (0,)), ((), ())),
                precision=HIGH,
                preferred_element_type=jnp.float32,
            )
            a_ref[hi:, :] = a_ref[hi:, :] - upd[hi:, :K]
            w_ref[hi:, :] = w_ref[hi:, :] - upd[hi:, K:]
    basis_ref[...] = w_ref[...].T


def factor(gram, xt):
    vm = pl.BlockSpec(memory_space=pltpu.VMEM)
    return pl.pallas_call(
        factor_kernel,
        out_shape=[
            jax.ShapeDtypeStruct((K, K), jnp.float32),
            jax.ShapeDtypeStruct((BS, K), jnp.float32),
        ],
        in_specs=[vm, vm],
        out_specs=[vm, vm],
        scratch_shapes=[pltpu.VMEM((K, K), jnp.float32), pltpu.VMEM((K, BS), jnp.float32)],
        name="factor",
    )(gram, xt)


def rank_in_owner(owner):
    n = owner.shape[-1]
    earlier = jnp.arange(n)[None, :] < jnp.arange(n)[:, None]
    same = owner[..., None, :] == owner[..., :, None]
    return jnp.sum((same & earlier).astype(jnp.int32), axis=-1)


def per_device(block_values, block_columns, row_counts, sketch):
    z, x, core = lax.axis_index("z"), lax.axis_index("x"), lax.axis_index("core")
    blocks = sketch.reshape(2, BPD // 2, BS, K)
    have = {0: [sketch.reshape(BPD, BS, K)]}
    fwd = {0: [blocks[0], blocks[1]]}
    bwd = {0: [blocks[0], blocks[1]]}
    for step in range(1, 5):
        fwd[step] = [None, None]
        bwd[step] = [None, None]
        for h in range(2):
            if step < 4 or h == 0:
                fwd[step][h] = lax.ppermute(fwd[step - 1][h], "z", ring(NZ, 1))
            if step < 4 or h == 1:
                bwd[step][h] = lax.ppermute(bwd[step - 1][h], "z", ring(NZ, -1))
        if step < 4:
            have[NZ - step] = fwd[step]
            have[step] = bwd[step]
        else:
            have[4] = [fwd[4][0], bwd[4][1]]

    slots = BR * S
    live = jnp.arange(S, dtype=jnp.int32)[None, :] < row_counts
    meta = jnp.where(live, block_columns, -1).reshape(slots)
    ids = jnp.arange(slots, dtype=jnp.int32)
    own = meta // BPD
    dist_z = (own // NX - z) % NZ
    dist_x = (own % NX - x) % NX
    owner = jnp.where(meta < 0, NX * NZ, dist_x * NZ + dist_z)
    place = owner * CAP + rank_in_owner(owner)
    spots = jnp.arange(NX * NZ * CAP, dtype=jnp.int32)
    wanted = jnp.sum(jnp.where(place[:, None] == spots[None, :], ids[:, None], 0), axis=0)
    flat_values = block_values.reshape(slots, BS, BS)
    metas = [meta.reshape(2, 128)]
    for dx in range(1, NX):
        metas.append(lax.ppermute(metas[0], "x", ring(NX, dx)))
    wanted, metas = lax.optimization_barrier((wanted, metas))
    metas = [m.reshape(slots) for m in metas]
    vals = []
    for dx in range(NX):
        part = wanted[dx * NZ * CAP : (dx + 1) * NZ * CAP]
        sent = flat_values.at[part].get(mode="promise_in_bounds")
        if dx:
            sent = lax.ppermute(sent, "x", ring(NX, dx))
        vals.append(sent.reshape(NZ, CAP, BS, BS))

    got = jnp.stack(metas)
    own = got // BPD
    match = (got >= 0) & (own % NX == x)
    dist = jnp.where(match, (own // NX - z) % NZ, NZ)
    rank = rank_in_owner(dist)
    hits = (dist[:, :, None] == jnp.arange(NZ)[None, None, :]).astype(jnp.int32)
    counts = jnp.sum(hits, axis=1)
    offsets = jnp.cumsum(counts, axis=0) - counts
    number = jnp.sum(counts, axis=0)
    shift = jnp.arange(NX, dtype=jnp.int32)[:, None]
    source = (x - shift) % NX
    entry = jnp.sum(hits * offsets[:, None, :], axis=2) + rank
    where = jnp.where(match, dist * ENTRIES + entry, -1).reshape(-1)
    block_row = (ids // S)[None, :]
    row = ((block_row % NC) ^ core) * (ROWS // 2) + source * NY + block_row // NC
    packed = shift * CAP + rank + 64 * (got % BPD) + 2048 * row
    dummy = 2048 * ROWS
    spots = jnp.arange(NZ * ENTRIES, dtype=jnp.int32)
    table = dummy + jnp.sum(
        jnp.where(where[:, None] == spots[None, :], packed.reshape(-1)[:, None] - dummy, 0), axis=0
    )

    prev = None
    groups = [(0, 1, 7, 2, 6), (3, 5), (4,)]
    for n, ds in enumerate(groups):
        last = n == len(groups) - 1
        prev = products(ds, table, number, vals, [have[d] for d in ds], prev, last)
        if not last:
            prev = prev[0]
    mine, other = prev
    half = mine + lax.ppermute(other, "core", ring(NC, 1))
    image = jnp.sum(lax.all_to_all(half, ("x", "y"), 0, 0, tiled=True), axis=0)

    gram = lax.dot_general(
        image, image, (((0,), (0,)), ((), ())), precision=HIGH, preferred_element_type=jnp.float32
    )
    plane = ("x", "y", "core")
    n_plane = NX * NY * NC
    piece = K // n_plane
    gram = gram.reshape(n_plane, piece, K)
    part = jnp.sum(lax.all_to_all(gram, plane, 0, 0, tiled=True), axis=0)
    part = jnp.broadcast_to(part[None], (NZ, piece, K))
    part = jnp.sum(lax.all_to_all(part, "z", 0, 0, tiled=True), axis=0) / (NZ * n_plane * BS)
    part = jnp.broadcast_to(part[None], (n_plane, piece, K))
    gram = lax.all_to_all(part, plane, 0, 0, tiled=True).reshape(K, K)
    triangle, basis = factor(gram, image.T)
    return basis, triangle


def solution(mesh):
    axes = ("z", "x", "y", "core")
    fine = Mesh(mesh.devices.reshape(NZ, NX, NY, NC), axes)
    rows, cols = ("z", "x"), ("y", "core")
    return jax.shard_map(
        per_device,
        mesh=fine,
        in_specs=(P(rows, cols, None, None), P(rows, cols), P(rows, cols), P(axes, None)),
        out_specs=(P(axes, None), P()),
        check_vma=False,
    )
```

```python
import functools

import jax
import jax.numpy as jnp
from jax import lax
from jax.experimental import pallas as pl
from jax.experimental.pallas import tpu as pltpu
from jax.sharding import Mesh
from jax.sharding import PartitionSpec as P

NZ, NX, NY, NC = 8, 4, 4, 2
CAP = 12
FULL = NZ * CAP
FIRST = 64
REST = FULL - FIRST
BR, S, BS, K = 8, 32, 128, 256
BPD = 32
ENTRIES = NX * CAP
ROWS = NX * BR
HIGH = lax.Precision.HIGHEST


def ring(n, shift):
    return [(i, (i + shift) % n) for i in range(n)]


def pack_kernel(index, values, *refs):
    outs, (buf, gsem, osem) = refs[:NX], refs[NX:]
    order = (2, 1, 3, 0)
    for dx in order:

        def fetch(i, carry, dx=dx):
            pltpu.make_async_copy(
                values.at[index[dx * FIRST + i]], buf.at[dx, i], gsem.at[dx]
            ).start()
            return carry

        lax.fori_loop(0, FIRST, fetch, 0, unroll=8)
    stores = []
    for dx in order:
        pltpu.make_async_copy(values.at[pl.ds(0, FIRST)], buf.at[dx], gsem.at[dx]).wait()
        stores.append(pltpu.make_async_copy(buf.at[dx], outs[dx], osem.at[dx]))
        stores[-1].start()
    for c in stores:
        c.wait()


def pack(index, values):
    anyspec = pl.BlockSpec(memory_space=pl.ANY)
    return pl.pallas_call(
        pack_kernel,
        out_shape=[jax.ShapeDtypeStruct((FIRST, BS, BS), jnp.bfloat16)] * NX,
        grid_spec=pltpu.PrefetchScalarGridSpec(
            num_scalar_prefetch=1,
            grid=(1,),
            in_specs=[anyspec],
            out_specs=[anyspec] * NX,
            scratch_shapes=[
                pltpu.VMEM((NX, FIRST, BS, BS), jnp.bfloat16),
                pltpu.SemaphoreType.DMA((NX,)),
                pltpu.SemaphoreType.DMA((NX,)),
            ],
        ),
        compiler_params=pltpu.CompilerParams(vmem_limit_bytes=16 << 20),
        cost_estimate=pl.CostEstimate(
            flops=0, bytes_accessed=2 * NX * FIRST * BS * BS * 2, transcendentals=0
        ),
        name="pack",
    )(index, values)


def products_kernel(ds, halves, window, first, last, *refs):
    refs = list(refs)
    tbl, num = refs[0], refs[1]
    whole = window == FULL
    vals = refs[2 : 2 + NX]
    pos = 2 + NX
    if whole:
        more = refs[pos : pos + NX]
        pos += NX
    tabs = []
    for h in halves:
        tabs.append(refs[pos : pos + h])
        pos += h
    if not first:
        prev = refs[pos]
        pos += 1
    nouts = 2 if last else 1
    outs = refs[pos : pos + nouts]
    vb, tb, acc, vsem, tsem, psem, msem = refs[pos + nouts :]
    size = min(window, FIRST)
    loads = [
        pltpu.make_async_copy(
            vals[dx].at[pl.ds(0, size)], vb.at[dx, pl.ds(0, size)], vsem.at[dx]
        )
        for dx in range(NX)
    ]
    for c in loads:
        c.start()
    waits = []
    for i, d in enumerate(ds):
        part = BPD // halves[i]
        waits.append(
            [
                pltpu.make_async_copy(tabs[i][h], tb.at[i, pl.ds(h * part, part)], tsem.at[i, h])
                for h in range(halves[i])
            ]
        )
        for c in waits[i]:
            c.start()
    if first:
        acc[...] = jnp.zeros_like(acc)
    else:
        load = pltpu.make_async_copy(prev, acc.at[pl.ds(0, ROWS)], psem.at[0])
        load.start()
        load.wait()
    for c in loads:
        c.wait()
    if whole:

        @pl.when(num[NZ] > FIRST)
        def _():
            for dx in range(NX):
                c = pltpu.make_async_copy(more[dx], vb.at[dx, pl.ds(FIRST, REST)], msem)
                c.start()
                c.wait()

    for i in range(len(ds)):
        for c in waits[i]:
            c.wait()

    def one_distance(i, carry):
        d = ds[0]
        for k in range(1, len(ds)):
            d = jnp.where(i == k, ds[k], d)

        def step(j, carry):
            for u in range(4):
                entry = tbl[d * ENTRIES + j * 4 + u]
                p = jnp.bitwise_and(entry, 127)
                dx = jnp.bitwise_and(lax.shift_right_logical(entry, 7), 3)
                t = jnp.bitwise_and(lax.shift_right_logical(entry, 9), 31)
                row = lax.shift_right_logical(entry, 14)
                acc[row] += jnp.dot(
                    vb[dx, p], tb[i, t], preferred_element_type=jnp.float32
                )
            return carry

        return lax.fori_loop(0, (num[d] + 3) // 4, step, carry)

    lax.fori_loop(0, len(ds), one_distance, 0)
    size = ROWS // nouts
    stores = [
        pltpu.make_async_copy(acc.at[pl.ds(o * size, size)], outs[o], psem.at[o])
        for o in range(nouts)
    ]
    for c in stores:
        c.start()
    for c in stores:
        c.wait()


def products(ds, window, tbl, num, vals, more, tabs, prev, last):
    halves = tuple(len(t) for t in tabs)
    first = prev is None
    args = list(vals) + (list(more) if window == FULL else [])
    args += [a for t in tabs for a in t] + ([] if first else [prev])
    shape = (ROWS // 2 if last else ROWS, BS, K)
    out = [jax.ShapeDtypeStruct(shape, jnp.float32)] * (2 if last else 1)
    anyspec = pl.BlockSpec(memory_space=pl.ANY)
    nd = len(ds)
    return pl.pallas_call(
        functools.partial(products_kernel, ds, halves, window, first, last),
        out_shape=out,
        grid_spec=pltpu.PrefetchScalarGridSpec(
            num_scalar_prefetch=2,
            grid=(1,),
            in_specs=[anyspec] * len(args),
            out_specs=[anyspec] * len(out),
            scratch_shapes=[
                pltpu.VMEM((NX, window, BS, BS), jnp.bfloat16),
                pltpu.VMEM((nd, BPD, BS, K), jnp.bfloat16),
                pltpu.VMEM((ROWS + 1, BS, K), jnp.float32),
                pltpu.SemaphoreType.DMA((NX,)),
                pltpu.SemaphoreType.DMA((nd, 2)),
                pltpu.SemaphoreType.DMA((2,)),
                pltpu.SemaphoreType.DMA,
            ],
        ),
        compiler_params=pltpu.CompilerParams(vmem_limit_bytes=40 << 20),
        cost_estimate=pl.CostEstimate(
            flops=nd * 20 * 2 * BS * BS * K,
            bytes_accessed=nd * BPD * BS * K * 2 + NX * window * BS * BS * 2 + 2 * ROWS * BS * K * 4,
            transcendentals=0,
        ),
    )(tbl, num, *args)


HB = 64


def factor_block(d):
    groups = [d[8 * g : 8 * g + 8, :] for g in range(8)]
    sub = lax.broadcasted_iota(jnp.int32, (8, 128), 0)
    for p in range(8):
        r = groups[p]
        cols = [jnp.broadcast_to(r[:, 8 * p + k : 8 * p + k + 1], (8, 128)) for k in range(8)]
        a = [
            [jnp.broadcast_to(cols[k][i : i + 1, :], (8, 128)) if i <= k else None for k in range(8)]
            for i in range(8)
        ]
        rs = [None] * 8
        rows = []
        for i in range(8):
            piv = a[i][i]
            y = lax.rsqrt(piv)
            rs[i] = y * (1.5 - 0.5 * (piv * y) * y)
            for k in range(i + 1, 8):
                a[i][k] = a[i][k] * rs[i]
            for k in range(i + 1, 8):
                for l in range(k, 8):
                    a[k][l] = a[k][l] - a[i][k] * a[i][l]
            row = jnp.broadcast_to(r[i : i + 1, :], (8, 128))
            for k in range(i):
                row = row - a[k][i] * rows[k]
            rows.append(row * rs[i])
        for g in range(p + 1, 8):
            cur = groups[g]
            mult = []
            for i in range(8):
                m = jnp.broadcast_to(cur[:, 8 * p + i : 8 * p + i + 1], (8, 128))
                for k in range(i):
                    m = m - mult[k] * a[k][i]
                mult.append(m * rs[i])
            for i in range(8):
                cur = cur - mult[i] * rows[i]
            groups[g] = cur
        new = rows[0]
        for i in range(1, 8):
            new = jnp.where(sub == i, rows[i], new)
        groups[p] = new
    return jnp.concatenate(groups, axis=0)


def factor_kernel(g_ref, xt_ref, tri_ref, basis_ref, a_ref, w_ref):
    a_ref[...] = g_ref[...]
    w_ref[...] = xt_ref[...]
    lane = lax.broadcasted_iota(jnp.int32, (HB, 128), 1)
    srow = lax.broadcasted_iota(jnp.int32, (HB, 128), 0)
    eye = jnp.where(lane - HB == srow, 1.0, 0.0).astype(jnp.float32)
    low = lane < HB
    rown = lax.broadcasted_iota(jnp.int32, (HB, K), 0)
    coln = lax.broadcasted_iota(jnp.int32, (HB, K), 1)
    for b in range(K // HB):
        lo, hi = b * HB, (b + 1) * HB
        tile = a_ref[lo:hi, 128 * (b // 2) : 128 * (b // 2) + 128]
        if b % 2:
            tile = pltpu.roll(tile, HB, 1)
        res = factor_block(jnp.where(low, tile, eye))
        inv = jnp.where(low, 0.0, res)
        zero = jnp.zeros((HB, K + BS), jnp.float32)
        both = jnp.concatenate([a_ref[lo:hi, :], w_ref[lo:hi, :]], axis=1)
        out = jnp.dot(
            inv,
            jnp.concatenate([zero, both], axis=0),
            precision=HIGH,
            preferred_element_type=jnp.float32,
        )
        upper = jnp.where(coln >= rown + lo, out[:, :K], 0.0)
        tri_ref[lo:hi, :] = upper
        w_ref[lo:hi, :] = out[:, K:]
        if hi < K:
            new = jnp.concatenate([upper, out[:, K:]], axis=1)
            upd = lax.dot_general(
                upper,
                new,
                (((0,), (0,)), ((), ())),
                precision=HIGH,
                preferred_element_type=jnp.float32,
            )
            a_ref[hi:, :] = a_ref[hi:, :] - upd[hi:, :K]
            w_ref[hi:, :] = w_ref[hi:, :] - upd[hi:, K:]
    basis_ref[...] = w_ref[...].T


def factor(gram, xt):
    vm = pl.BlockSpec(memory_space=pltpu.VMEM)
    return pl.pallas_call(
        factor_kernel,
        out_shape=[
            jax.ShapeDtypeStruct((K, K), jnp.float32),
            jax.ShapeDtypeStruct((BS, K), jnp.float32),
        ],
        in_specs=[vm, vm],
        out_specs=[vm, vm],
        scratch_shapes=[pltpu.VMEM((K, K), jnp.float32), pltpu.VMEM((K, BS), jnp.float32)],
        name="factor",
    )(gram, xt)


def hand_on_kernel(x_ref, o_ref):
    o_ref[...] = x_ref[...]


def hand_on(x):
    vm = pl.BlockSpec(memory_space=pltpu.VMEM)
    return pl.pallas_call(
        hand_on_kernel,
        out_shape=jax.ShapeDtypeStruct(x.shape, x.dtype),
        in_specs=[vm],
        out_specs=vm,
        name="hand_on",
    )(x)


def rank_in_group(group, order):
    n = group.shape[-1]
    key = order * n + jnp.arange(n, dtype=jnp.int32)
    same = group[..., None, :] == group[..., :, None]
    before = key[..., None, :] < key[..., :, None]
    return jnp.sum((same & before).astype(jnp.int32), axis=-1)


def distance_order(d):
    return jnp.where(d == 4, 0, jnp.where(d == 3, 1, jnp.where(d == 5, 2, d + 3)))


def one_device(block_values, block_columns, row_counts, sketch):
    z, x, core = lax.axis_index("z"), lax.axis_index("x"), lax.axis_index("core")
    blocks = sketch.reshape(2, BPD // 2, BS, K)
    have = {0: [sketch.reshape(BPD, BS, K)]}
    fwd = {1: [lax.ppermute(blocks[h], "z", ring(NZ, 1)) for h in range(2)]}
    bwd = {1: [lax.ppermute(blocks[h], "z", ring(NZ, -1)) for h in range(2)]}

    slots = BR * S
    live = jnp.arange(S, dtype=jnp.int32)[None, :] < row_counts
    meta = jnp.where(live, block_columns, -1).reshape(slots)
    ids = jnp.arange(slots, dtype=jnp.int32)
    own = meta // BPD
    dist_z = (own // NX - z) % NZ
    dist_x = jnp.where(meta < 0, NX, (own % NX - x) % NX)
    place = dist_x * FULL + rank_in_group(dist_x, distance_order(dist_z))
    spots = jnp.arange(NX * FULL, dtype=jnp.int32)
    wanted = jnp.sum(jnp.where(place[:, None] == spots[None, :], ids[:, None], 0), axis=0)
    wanted = wanted.reshape(NX, FULL)
    flat_values = block_values.reshape(slots, BS, BS)
    metas = [meta.reshape(2, 128)]
    for dx in range(1, NX):
        metas.append(lax.ppermute(metas[0], "x", ring(NX, dx)))
    wanted, metas = lax.optimization_barrier((wanted, metas))
    vals = list(pack(wanted[:, :FIRST].reshape(-1), flat_values))
    for dx in range(1, NX):
        vals[dx] = lax.ppermute(vals[dx], "x", ring(NX, dx))

    for step in range(1, 5):
        if step > 1:
            fwd[step] = [None, None]
            bwd[step] = [None, None]
            for h in range(2):
                if step < 4 or h == 0:
                    fwd[step][h] = lax.ppermute(fwd[step - 1][h], "z", ring(NZ, 1))
                if step < 4 or h == 1:
                    bwd[step][h] = lax.ppermute(bwd[step - 1][h], "z", ring(NZ, -1))
        if step < 4:
            have[NZ - step] = fwd[step]
            have[step] = bwd[step]
        else:
            have[4] = [fwd[4][0], bwd[4][1]]

    got = hand_on(jnp.stack([m.reshape(slots) for m in metas]))
    own = got // BPD
    shift = jnp.arange(NX, dtype=jnp.int32)[:, None]
    source = (x - shift) % NX
    towards = jnp.where(got < 0, NX, own % NX)
    match = towards == x
    dist = (own // NX - z) % NZ
    place = rank_in_group(towards, distance_order(dist))
    dist = jnp.where(match, dist, NZ)
    rank = rank_in_group(dist, jnp.zeros_like(dist))
    hits = (dist[:, :, None] == jnp.arange(NZ)[None, None, :]).astype(jnp.int32)
    counts = jnp.sum(hits, axis=1)
    offsets = jnp.cumsum(counts, axis=0) - counts
    number = jnp.sum(counts, axis=0)
    entry = jnp.sum(hits * offsets[:, None, :], axis=2) + rank
    where = jnp.where(match, dist * ENTRIES + entry, -1).reshape(-1)
    block_row = (ids // S)[None, :]
    row = ((block_row % NC) ^ core) * (ROWS // 2) + source * NY + block_row // NC
    packed = place + 128 * shift + 512 * (got % BPD) + 16384 * row
    dummy = 16384 * ROWS
    spots = jnp.arange(NZ * ENTRIES, dtype=jnp.int32)
    table = dummy + jnp.sum(
        jnp.where(where[:, None] == spots[None, :], packed.reshape(-1)[:, None] - dummy, 0), axis=0
    )

    longest = jnp.max(jnp.where(got >= 0, place, -1)) + 1

    def second_part():
        parts = []
        for dx in range(NX):
            sent = flat_values.at[wanted[dx, FIRST:]].get(mode="promise_in_bounds")
            parts.append(lax.ppermute(sent, "x", ring(NX, dx)) if dx else sent)
        return tuple(parts)

    def no_second_part():
        return (jnp.zeros((REST, BS, BS), jnp.bfloat16),) * NX

    more = lax.cond(longest > FIRST, second_part, no_second_part)
    number = jnp.concatenate([number, longest[None]])

    prev = None
    groups = [((0, 1, 7, 2, 6), FULL), ((3, 5), 3 * CAP), ((4,), CAP)]
    for n, (ds, window) in enumerate(groups):
        last = n == len(groups) - 1
        tabs = [have[d] for d in ds]
        prev = products(ds, window, table, number, vals, more, tabs, prev, last)
        if not last:
            prev = prev[0]
    mine, other = prev
    half = mine + lax.ppermute(other, "core", ring(NC, 1))
    image = jnp.sum(lax.all_to_all(half, ("x", "y"), 0, 0, tiled=True), axis=0)

    gram = lax.dot_general(
        image, image, (((0,), (0,)), ((), ())), precision=HIGH, preferred_element_type=jnp.float32
    )
    plane = ("x", "y", "core")
    n_plane = NX * NY * NC
    piece = K // n_plane
    gram = gram.reshape(n_plane, piece, K)
    part = jnp.sum(lax.all_to_all(gram, plane, 0, 0, tiled=True), axis=0)
    part = jnp.broadcast_to(part[None], (NZ, piece, K))
    part = jnp.sum(lax.all_to_all(part, "z", 0, 0, tiled=True), axis=0) / (NZ * n_plane * BS)
    part = jnp.broadcast_to(part[None], (n_plane, piece, K))
    gram = lax.all_to_all(part, plane, 0, 0, tiled=True).reshape(K, K)
    triangle, basis = factor(gram, image.T)
    return basis, triangle


def solution(mesh):
    axes = ("z", "x", "y", "core")
    fine = Mesh(mesh.devices.reshape(NZ, NX, NY, NC), axes)
    rows, cols = ("z", "x"), ("y", "core")
    return jax.shard_map(
        one_device,
        mesh=fine,
        in_specs=(P(rows, cols, None, None), P(rows, cols), P(rows, cols), P(axes, None)),
        out_specs=(P(axes, None), P()),
        check_vma=False,
    )
```

```python
import functools

import jax
import jax.numpy as jnp
from jax import lax
from jax.experimental import pallas as pl
from jax.experimental.pallas import tpu as pltpu
from jax.sharding import Mesh
from jax.sharding import PartitionSpec as P

NZ, NX, NY, NC = 8, 4, 4, 2
CAP = 12
FULL = NZ * CAP
FIRST = 72
REST = FULL - FIRST
BR, S, BS, K = 8, 32, 128, 256
BPD = 32
ENTRIES = NX * CAP
ROWS = NX * BR
HIGH = lax.Precision.HIGHEST


def ring(n, shift):
    return [(i, (i + shift) % n) for i in range(n)]


def split_kernel(x_ref, near, far, buf, isem, osem):
    step = BPD // 4
    loads, stores = [], []
    for c in range(4):
        out = (near, far)[c // 2].at[pl.ds(c % 2 * step, step)]
        loads.append(pltpu.make_async_copy(x_ref.at[pl.ds(c * step, step)], buf.at[c], isem.at[c]))
        stores.append(pltpu.make_async_copy(buf.at[c], out, osem.at[c]))
    for c in loads:
        c.start()
    for load, store in zip(loads, stores):
        load.wait()
        store.start()
    for c in stores:
        c.wait()


def split(blocks):
    half = jax.ShapeDtypeStruct((BPD // 2, BS, K), jnp.bfloat16)
    anyspec = pl.BlockSpec(memory_space=pl.ANY)
    return pl.pallas_call(
        split_kernel,
        out_shape=[half, half],
        in_specs=[anyspec],
        out_specs=[anyspec, anyspec],
        scratch_shapes=[
            pltpu.VMEM((4, BPD // 4, BS, K), jnp.bfloat16),
            pltpu.SemaphoreType.DMA((4,)),
            pltpu.SemaphoreType.DMA((4,)),
        ],
        compiler_params=pltpu.CompilerParams(vmem_limit_bytes=60 << 20),
        cost_estimate=pl.CostEstimate(
            flops=0, bytes_accessed=2 * BPD * BS * K * 2, transcendentals=0
        ),
        name="split",
    )(blocks)


def pack_kernel(n, index, values, *refs):
    outs, (buf, gsem, osem) = refs[:n], refs[n:]
    for m in range(n):

        def fetch(i, carry, m=m):
            pltpu.make_async_copy(
                values.at[index[m * FIRST + i]], buf.at[m, i], gsem.at[m]
            ).start()
            return carry

        lax.fori_loop(0, FIRST, fetch, 0, unroll=8)
    stores = []
    for m in range(n):
        pltpu.make_async_copy(values.at[pl.ds(0, FIRST)], buf.at[m], gsem.at[m]).wait()
        stores.append(pltpu.make_async_copy(buf.at[m], outs[m], osem.at[m]))
        stores[-1].start()
    for c in stores:
        c.wait()


def pack(index, values):
    n = index.shape[0]
    anyspec = pl.BlockSpec(memory_space=pl.ANY)
    return pl.pallas_call(
        functools.partial(pack_kernel, n),
        out_shape=[jax.ShapeDtypeStruct((FIRST, BS, BS), jnp.bfloat16)] * n,
        grid_spec=pltpu.PrefetchScalarGridSpec(
            num_scalar_prefetch=1,
            grid=(1,),
            in_specs=[anyspec],
            out_specs=[anyspec] * n,
            scratch_shapes=[
                pltpu.VMEM((n, FIRST, BS, BS), jnp.bfloat16),
                pltpu.SemaphoreType.DMA((n,)),
                pltpu.SemaphoreType.DMA((n,)),
            ],
        ),
        compiler_params=pltpu.CompilerParams(vmem_limit_bytes=16 << 20),
        cost_estimate=pl.CostEstimate(
            flops=0, bytes_accessed=2 * n * FIRST * BS * BS * 2, transcendentals=0
        ),
    )(index.reshape(-1), values)


def products_kernel(ds, halves, window, first, *refs):
    refs = list(refs)
    tbl, num = refs[0], refs[1]
    whole = window == FULL
    vals = refs[2 : 2 + NX]
    pos = 2 + NX
    if whole:
        more = refs[pos : pos + NX]
        pos += NX
    tabs = []
    for h in halves:
        tabs.append(refs[pos : pos + h])
        pos += h
    if not first:
        pos += 2
    rows = refs[pos : pos + 2]
    vb, tb, vsem, tsem, msem = refs[pos + 2 :]
    size = min(window, FIRST)
    loads = [
        pltpu.make_async_copy(
            vals[dx].at[pl.ds(0, size)], vb.at[dx, pl.ds(0, size)], vsem.at[dx]
        )
        for dx in range(NX)
    ]
    for i in range(len(ds)):
        part = BPD // halves[i]
        loads += [
            pltpu.make_async_copy(tabs[i][h], tb.at[i, pl.ds(h * part, part)], tsem.at[i, h])
            for h in range(halves[i])
        ]
    for c in loads:
        c.start()
    vb[0, window] = jnp.zeros((BS, BS), jnp.bfloat16)
    for h in range(2):
        if first:
            rows[h][...] = jnp.zeros_like(rows[h])
    if whole:

        @pl.when(num[2 * NZ] > FIRST)
        def _():
            for dx in range(NX):
                c = pltpu.make_async_copy(more[dx], vb.at[dx, pl.ds(FIRST, REST)], msem)
                c.start()
                c.wait()

    for c in loads:
        c.wait()

    def one_distance(i, carry):
        d = ds[0]
        for k in range(1, len(ds)):
            d = jnp.where(i == k, ds[k], d)
        for h in range(2):
            which = 2 * d + h

            def step(j, carry, h=h, which=which):
                for u in range(4):
                    entry = tbl[which * ENTRIES + j * 4 + u]
                    p = jnp.minimum(jnp.bitwise_and(entry, 127), window)
                    dx = jnp.bitwise_and(lax.shift_right_logical(entry, 7), 3)
                    t = jnp.bitwise_and(lax.shift_right_logical(entry, 9), 31)
                    row = lax.shift_right_logical(entry, 14)
                    rows[h][row] += jnp.dot(
                        vb[dx, p], tb[i, t], preferred_element_type=jnp.float32
                    )
                return carry

            lax.fori_loop(0, (num[which] + 3) // 4, step, 0)
        return carry

    lax.fori_loop(0, len(ds), one_distance, 0)


def products(ds, window, tbl, num, vals, more, tabs, prev):
    halves = tuple(len(t) for t in tabs)
    first = prev is None
    args = list(vals) + (list(more) if window == FULL else [])
    args += [a for t in tabs for a in t]
    smem = pl.BlockSpec(memory_space=pltpu.SMEM)
    vmem = pl.BlockSpec(memory_space=pltpu.VMEM)
    anyspec = pl.BlockSpec(memory_space=pl.ANY)
    specs = [smem, smem] + [anyspec] * len(args)
    aliases = {}
    if not first:
        aliases = {len(specs): 0, len(specs) + 1: 1}
        args += list(prev)
        specs += [vmem, vmem]
    nd = len(ds)
    return pl.pallas_call(
        functools.partial(products_kernel, ds, halves, window, first),
        out_shape=[jax.ShapeDtypeStruct((ROWS // 2, BS, K), jnp.float32)] * 2,
        in_specs=specs,
        out_specs=[vmem, vmem],
        scratch_shapes=[
            pltpu.VMEM((NX, window + 1, BS, BS), jnp.bfloat16),
            pltpu.VMEM((nd, BPD, BS, K), jnp.bfloat16),
            pltpu.SemaphoreType.DMA((NX,)),
            pltpu.SemaphoreType.DMA((nd, 2)),
            pltpu.SemaphoreType.DMA,
        ],
        input_output_aliases=aliases,
        compiler_params=pltpu.CompilerParams(vmem_limit_bytes=40 << 20),
        cost_estimate=pl.CostEstimate(
            flops=nd * 20 * 2 * BS * BS * K,
            bytes_accessed=nd * BPD * BS * K * 2 + NX * window * BS * BS * 2,
            transcendentals=0,
        ),
    )(tbl, num, *args)


HB = 64


def factor_block(d):
    groups = [d[8 * g : 8 * g + 8, :] for g in range(8)]
    sub = lax.broadcasted_iota(jnp.int32, (8, 128), 0)
    for p in range(8):
        r = groups[p]
        cols = [jnp.broadcast_to(r[:, 8 * p + k : 8 * p + k + 1], (8, 128)) for k in range(8)]
        a = [
            [jnp.broadcast_to(cols[k][i : i + 1, :], (8, 128)) if i <= k else None for k in range(8)]
            for i in range(8)
        ]
        rs = [None] * 8
        rows = []
        for i in range(8):
            rs[i] = lax.rsqrt(a[i][i])
            for k in range(i + 1, 8):
                a[i][k] = a[i][k] * rs[i]
            for k in range(i + 1, 8):
                for l in range(k, 8):
                    a[k][l] = a[k][l] - a[i][k] * a[i][l]
            row = jnp.broadcast_to(r[i : i + 1, :], (8, 128))
            for k in range(i):
                row = row - a[k][i] * rows[k]
            rows.append(row * rs[i])
        for g in range(p + 1, 8):
            cur = groups[g]
            mult = []
            for i in range(8):
                m = jnp.broadcast_to(cur[:, 8 * p + i : 8 * p + i + 1], (8, 128))
                for k in range(i):
                    m = m - mult[k] * a[k][i]
                mult.append(m * rs[i])
            for i in range(8):
                cur = cur - mult[i] * rows[i]
            groups[g] = cur
        new = rows[0]
        for i in range(1, 8):
            new = jnp.where(sub == i, rows[i], new)
        groups[p] = new
    return jnp.concatenate(groups, axis=0)


def factor_kernel(g_ref, xt_ref, tri_ref, basis_ref, a_ref, w_ref):
    a_ref[...] = g_ref[...]
    w_ref[...] = xt_ref[...]
    lane = lax.broadcasted_iota(jnp.int32, (HB, 128), 1)
    srow = lax.broadcasted_iota(jnp.int32, (HB, 128), 0)
    eye = jnp.where(lane - HB == srow, 1.0, 0.0).astype(jnp.float32)
    low = lane < HB
    rown = lax.broadcasted_iota(jnp.int32, (HB, K), 0)
    coln = lax.broadcasted_iota(jnp.int32, (HB, K), 1)
    for b in range(K // HB):
        lo, hi = b * HB, (b + 1) * HB
        tile = a_ref[lo:hi, 128 * (b // 2) : 128 * (b // 2) + 128]
        if b % 2:
            tile = pltpu.roll(tile, HB, 1)
        res = factor_block(jnp.where(low, tile, eye))
        inv = jnp.where(low, 0.0, res)
        left = lo // 128 * 128
        zero = jnp.zeros((HB, K - left + BS), jnp.float32)
        both = jnp.concatenate([a_ref[lo:hi, left:], w_ref[lo:hi, :]], axis=1)
        out = jnp.dot(
            inv,
            jnp.concatenate([zero, both], axis=0),
            precision=HIGH,
            preferred_element_type=jnp.float32,
        )
        upper = jnp.where((coln >= rown + lo)[:, left:], out[:, : K - left], 0.0)
        if left:
            tri_ref[lo:hi, :left] = jnp.zeros((HB, left), jnp.float32)
        tri_ref[lo:hi, left:] = upper
        w_ref[lo:hi, :] = out[:, K - left :]
        if hi < K:
            rest = hi // 128 * 128
            part = upper[:, rest - left :]
            new = jnp.concatenate([part, out[:, K - left :]], axis=1)
            upd = lax.dot_general(
                part,
                new,
                (((0,), (0,)), ((), ())),
                precision=HIGH,
                preferred_element_type=jnp.float32,
            )
            a_ref[hi:, rest:] = a_ref[hi:, rest:] - upd[hi - rest :, : K - rest]
            w_ref[hi:, :] = w_ref[hi:, :] - upd[hi - rest :, K - rest :]
    basis_ref[...] = w_ref[...].T


def factor(gram, xt):
    vm = pl.BlockSpec(memory_space=pltpu.VMEM)
    return pl.pallas_call(
        factor_kernel,
        out_shape=[
            jax.ShapeDtypeStruct((K, K), jnp.float32),
            jax.ShapeDtypeStruct((BS, K), jnp.float32),
        ],
        in_specs=[vm, vm],
        out_specs=[vm, vm],
        scratch_shapes=[pltpu.VMEM((K, K), jnp.float32), pltpu.VMEM((K, BS), jnp.float32)],
        name="factor",
    )(gram, xt)


def hand_on_kernel(x_ref, o_ref):
    o_ref[...] = x_ref[...]


def hand_on(x):
    vm = pl.BlockSpec(memory_space=pltpu.VMEM)
    return pl.pallas_call(
        hand_on_kernel,
        out_shape=jax.ShapeDtypeStruct(x.shape, x.dtype),
        in_specs=[vm],
        out_specs=vm,
        name="hand_on",
    )(x)


def rank_in_group(group, order):
    n = group.shape[-1]
    key = order * n + jnp.arange(n, dtype=jnp.int32)
    same = group[..., None, :] == group[..., :, None]
    before = key[..., None, :] < key[..., :, None]
    return jnp.sum((same & before).astype(jnp.int32), axis=-1)


def distance_order(d):
    return jnp.where(d == 4, 0, jnp.where(d == 3, 1, jnp.where(d == 5, 2, d + 3)))


def one_device(block_values, block_columns, row_counts, sketch):
    z, x, core = lax.axis_index("z"), lax.axis_index("x"), lax.axis_index("core")
    blocks = split(sketch.reshape(BPD, BS, K))
    have = {0: [sketch.reshape(BPD, BS, K)]}
    fwd = {1: [lax.ppermute(blocks[h], "z", ring(NZ, 1)) for h in range(2)]}
    bwd = {1: [lax.ppermute(blocks[h], "z", ring(NZ, -1)) for h in range(2)]}

    slots = BR * S
    live = jnp.arange(S, dtype=jnp.int32)[None, :] < row_counts
    meta = jnp.where(live, block_columns, -1).reshape(slots)
    ids = jnp.arange(slots, dtype=jnp.int32)
    own = meta // BPD
    dist_z = (own // NX - z) % NZ
    dist_x = jnp.where(meta < 0, NX, (own % NX - x) % NX)
    place = dist_x * FULL + rank_in_group(dist_x, distance_order(dist_z))
    spots = jnp.arange(NX * FULL, dtype=jnp.int32)
    wanted = jnp.sum(jnp.where(place[:, None] == spots[None, :], ids[:, None], 0), axis=0)
    wanted = wanted.reshape(NX, FULL)
    flat_values = block_values.reshape(slots, BS, BS)
    metas = [meta.reshape(2, 128)]
    for dx in range(1, NX):
        metas.append(lax.ppermute(metas[0], "x", ring(NX, dx)))
    wanted, metas = lax.optimization_barrier((wanted, metas))
    vals = [*pack(wanted[:1, :FIRST], flat_values), *pack(wanted[1:, :FIRST], flat_values)]
    for dx in range(1, NX):
        vals[dx] = lax.ppermute(vals[dx], "x", ring(NX, dx))

    for step in range(1, 5):
        if step > 1:
            fwd[step] = [None, None]
            bwd[step] = [None, None]
            for h in range(2):
                if step < 4 or h == 0:
                    fwd[step][h] = lax.ppermute(fwd[step - 1][h], "z", ring(NZ, 1))
                if step < 4 or h == 1:
                    bwd[step][h] = lax.ppermute(bwd[step - 1][h], "z", ring(NZ, -1))
        if step < 4:
            have[NZ - step] = fwd[step]
            have[step] = bwd[step]
        else:
            have[4] = [fwd[4][0], bwd[4][1]]

    metas[0] = hand_on(metas[0])
    got = jnp.stack([m.reshape(slots) for m in metas])
    own = got // BPD
    shift = jnp.arange(NX, dtype=jnp.int32)[:, None]
    source = (x - shift) % NX
    towards = jnp.where(got < 0, NX, own % NX)
    match = towards == x
    dist = (own // NX - z) % NZ
    place = rank_in_group(towards, distance_order(dist))
    block_row = (ids // S)[None, :]
    group = jnp.where(match, 2 * dist + ((block_row % NC) ^ core), 2 * NZ)
    rank = rank_in_group(group, jnp.zeros_like(group))
    hits = (group[:, :, None] == jnp.arange(2 * NZ)[None, None, :]).astype(jnp.int32)
    counts = jnp.sum(hits, axis=1)
    offsets = jnp.cumsum(counts, axis=0) - counts
    number = jnp.sum(counts, axis=0)
    entry = jnp.sum(hits * offsets[:, None, :], axis=2) + rank
    where = jnp.where(match, group * ENTRIES + entry, -1).reshape(-1)
    row = source * NY + block_row // NC
    packed = place + 128 * shift + 512 * (got % BPD) + 16384 * row
    filling = 127
    spots = jnp.arange(2 * NZ * ENTRIES, dtype=jnp.int32)
    table = filling + jnp.sum(
        jnp.where(where[:, None] == spots[None, :], packed.reshape(-1)[:, None] - filling, 0),
        axis=0,
    )

    longest = jnp.max(jnp.where(got >= 0, place, -1)) + 1

    def second_part():
        parts = []
        for dx in range(NX):
            sent = flat_values.at[wanted[dx, FIRST:]].get(mode="promise_in_bounds")
            parts.append(lax.ppermute(sent, "x", ring(NX, dx)) if dx else sent)
        return tuple(parts)

    def no_second_part():
        return (jnp.zeros((REST, BS, BS), jnp.bfloat16),) * NX

    more = lax.cond(longest > FIRST, second_part, no_second_part)
    number = jnp.concatenate([number, longest[None]])

    prev = None
    groups = [((0, 1, 7, 2, 6), FULL), ((3, 5), 3 * CAP), ((4,), CAP)]
    for ds, window in groups:
        prev = products(ds, window, table, number, vals, more, [have[d] for d in ds], prev)
    mine, other = prev
    half = mine + lax.ppermute(other, "core", ring(NC, 1))
    image = jnp.sum(lax.all_to_all(half, ("x", "y"), 0, 0, tiled=True), axis=0)

    gram = lax.dot_general(
        image, image, (((0,), (0,)), ((), ())), precision=HIGH, preferred_element_type=jnp.float32
    )
    plane = ("x", "y", "core")
    n_plane = NX * NY * NC
    piece = K // n_plane
    gram = gram.reshape(n_plane, piece, K)
    part = jnp.sum(lax.all_to_all(gram, plane, 0, 0, tiled=True), axis=0)
    part = jnp.broadcast_to(part[None], (NZ, piece, K))
    part = jnp.sum(lax.all_to_all(part, "z", 0, 0, tiled=True), axis=0) / (NZ * n_plane * BS)
    part = jnp.broadcast_to(part[None], (n_plane, piece, K))
    gram = lax.all_to_all(part, plane, 0, 0, tiled=True).reshape(K, K)
    triangle, basis = factor(gram, image.T)
    return basis, triangle


def solution(mesh):
    axes = ("z", "x", "y", "core")
    fine = Mesh(mesh.devices.reshape(NZ, NX, NY, NC), axes)
    rows, cols = ("z", "x"), ("y", "core")
    return jax.shard_map(
        one_device,
        mesh=fine,
        in_specs=(P(rows, cols, None, None), P(rows, cols), P(rows, cols), P(axes, None)),
        out_specs=(P(axes, None), P()),
        check_vma=False,
    )
```

```python
import functools

import jax
import jax.numpy as jnp
from jax import lax
from jax.experimental import pallas as pl
from jax.experimental.pallas import tpu as pltpu
from jax.sharding import Mesh
from jax.sharding import PartitionSpec as P

NZ, NX, NY, NC = 8, 4, 4, 2
CAP = 12
FULL = NZ * CAP
FIRST = 72
REST = FULL - FIRST
BR, S, BS, K = 8, 32, 128, 256
BPD = 32
ENTRIES = NX * CAP
ROWS = NX * BR
HIGH = lax.Precision.HIGHEST


def ring(n, shift):
    return [(i, (i + shift) % n) for i in range(n)]


def split_kernel(x_ref, near, far, buf, isem, osem):
    step = BPD // 4
    loads, stores = [], []
    for c in range(4):
        out = (near, far)[c // 2].at[pl.ds(c % 2 * step, step)]
        loads.append(pltpu.make_async_copy(x_ref.at[pl.ds(c * step, step)], buf.at[c], isem.at[c]))
        stores.append(pltpu.make_async_copy(buf.at[c], out, osem.at[c]))
    for c in loads:
        c.start()
    for load, store in zip(loads, stores):
        load.wait()
        store.start()
    for c in stores:
        c.wait()


def split(blocks):
    half = jax.ShapeDtypeStruct((BPD // 2, BS, K), jnp.bfloat16)
    anyspec = pl.BlockSpec(memory_space=pl.ANY)
    return pl.pallas_call(
        split_kernel,
        out_shape=[half, half],
        in_specs=[anyspec],
        out_specs=[anyspec, anyspec],
        scratch_shapes=[
            pltpu.VMEM((4, BPD // 4, BS, K), jnp.bfloat16),
            pltpu.SemaphoreType.DMA((4,)),
            pltpu.SemaphoreType.DMA((4,)),
        ],
        compiler_params=pltpu.CompilerParams(vmem_limit_bytes=60 << 20),
        cost_estimate=pl.CostEstimate(
            flops=0, bytes_accessed=2 * BPD * BS * K * 2, transcendentals=0
        ),
        name="split",
    )(blocks)


def pack_kernel(n, index, values, *refs):
    outs, (buf, gsem, osem) = refs[:n], refs[n:]
    for m in range(n):

        def fetch(i, carry, m=m):
            pltpu.make_async_copy(
                values.at[index[m * FIRST + i]], buf.at[m, i], gsem.at[m]
            ).start()
            return carry

        lax.fori_loop(0, FIRST, fetch, 0, unroll=8)
    stores = []
    for m in range(n):
        pltpu.make_async_copy(values.at[pl.ds(0, FIRST)], buf.at[m], gsem.at[m]).wait()
        stores.append(pltpu.make_async_copy(buf.at[m], outs[m], osem.at[m]))
        stores[-1].start()
    for c in stores:
        c.wait()


def pack(index, values):
    n = index.shape[0]
    anyspec = pl.BlockSpec(memory_space=pl.ANY)
    return pl.pallas_call(
        functools.partial(pack_kernel, n),
        out_shape=[jax.ShapeDtypeStruct((FIRST, BS, BS), jnp.bfloat16)] * n,
        grid_spec=pltpu.PrefetchScalarGridSpec(
            num_scalar_prefetch=1,
            grid=(1,),
            in_specs=[anyspec],
            out_specs=[anyspec] * n,
            scratch_shapes=[
                pltpu.VMEM((n, FIRST, BS, BS), jnp.bfloat16),
                pltpu.SemaphoreType.DMA((n,)),
                pltpu.SemaphoreType.DMA((n,)),
            ],
        ),
        compiler_params=pltpu.CompilerParams(vmem_limit_bytes=16 << 20),
        cost_estimate=pl.CostEstimate(
            flops=0, bytes_accessed=2 * n * FIRST * BS * BS * 2, transcendentals=0
        ),
    )(index.reshape(-1), values)


def products_kernel(ds, halves, window, first, *refs):
    refs = list(refs)
    tbl, num = refs[0], refs[1]
    whole = window == FULL
    vals = refs[2 : 2 + NX]
    pos = 2 + NX
    if whole:
        more = refs[pos : pos + NX]
        pos += NX
    tabs = []
    for h in halves:
        tabs.append(refs[pos : pos + h])
        pos += h
    if not first:
        pos += 2
    rows = refs[pos : pos + 2]
    vb, tb, vsem, tsem, msem = refs[pos + 2 :]
    size = min(window, FIRST)
    loads = [
        pltpu.make_async_copy(
            vals[dx].at[pl.ds(0, size)], vb.at[dx, pl.ds(0, size)], vsem.at[dx]
        )
        for dx in range(NX)
    ]
    for i in range(len(ds)):
        part = BPD // halves[i]
        loads += [
            pltpu.make_async_copy(tabs[i][h], tb.at[i, pl.ds(h * part, part)], tsem.at[i, h])
            for h in range(halves[i])
        ]
    for c in loads:
        c.start()
    vb[0, window] = jnp.zeros((BS, BS), jnp.bfloat16)
    for h in range(2):
        if first:
            rows[h][...] = jnp.zeros_like(rows[h])
    if whole:

        @pl.when(num[2 * NZ] > FIRST)
        def _():
            for dx in range(NX):
                c = pltpu.make_async_copy(more[dx], vb.at[dx, pl.ds(FIRST, REST)], msem)
                c.start()
                c.wait()

    for c in loads:
        c.wait()

    def one_distance(i, carry):
        d = ds[0]
        for k in range(1, len(ds)):
            d = jnp.where(i == k, ds[k], d)
        for h in range(2):
            which = 2 * d + h

            def step(j, carry, h=h, which=which):
                for u in range(4):
                    entry = tbl[which * ENTRIES + j * 4 + u]
                    p = jnp.minimum(jnp.bitwise_and(entry, 127), window)
                    dx = jnp.bitwise_and(lax.shift_right_logical(entry, 7), 3)
                    t = jnp.bitwise_and(lax.shift_right_logical(entry, 9), 31)
                    row = lax.shift_right_logical(entry, 14)
                    rows[h][row] += jnp.dot(
                        vb[dx, p], tb[i, t], preferred_element_type=jnp.float32
                    )
                return carry

            lax.fori_loop(0, (num[which] + 3) // 4, step, 0)
        return carry

    lax.fori_loop(0, len(ds), one_distance, 0)


def products(ds, window, tbl, num, vals, more, tabs, prev):
    halves = tuple(len(t) for t in tabs)
    first = prev is None
    args = list(vals) + (list(more) if window == FULL else [])
    args += [a for t in tabs for a in t]
    smem = pl.BlockSpec(memory_space=pltpu.SMEM)
    vmem = pl.BlockSpec(memory_space=pltpu.VMEM)
    anyspec = pl.BlockSpec(memory_space=pl.ANY)
    specs = [smem, smem] + [anyspec] * len(args)
    aliases = {}
    if not first:
        aliases = {len(specs): 0, len(specs) + 1: 1}
        args += list(prev)
        specs += [vmem, vmem]
    nd = len(ds)
    return pl.pallas_call(
        functools.partial(products_kernel, ds, halves, window, first),
        out_shape=[jax.ShapeDtypeStruct((ROWS // 2, BS, K), jnp.float32)] * 2,
        in_specs=specs,
        out_specs=[vmem, vmem],
        scratch_shapes=[
            pltpu.VMEM((NX, window + 1, BS, BS), jnp.bfloat16),
            pltpu.VMEM((nd, BPD, BS, K), jnp.bfloat16),
            pltpu.SemaphoreType.DMA((NX,)),
            pltpu.SemaphoreType.DMA((nd, 2)),
            pltpu.SemaphoreType.DMA,
        ],
        input_output_aliases=aliases,
        compiler_params=pltpu.CompilerParams(vmem_limit_bytes=40 << 20),
        cost_estimate=pl.CostEstimate(
            flops=nd * 20 * 2 * BS * BS * K,
            bytes_accessed=nd * BPD * BS * K * 2 + NX * window * BS * BS * 2,
            transcendentals=0,
        ),
    )(tbl, num, *args)


HB = 64


def spread_kernel(mine, theirs, *outs):
    top, bottom = outs[:NX], outs[NX:]
    half = BS // 2
    for r in range(NX):

        def step(j, carry, r=r):
            i = NY * r + j
            top[r][j] = mine[i, :half] + theirs[i, :half]
            i = NY * j + r
            bottom[r][j] = mine[i, half:] + theirs[i, half:]
            return carry

        lax.fori_loop(0, NX, step, 0)


def add_up_kernel(*refs):
    outs = refs[2 * NX :]
    for side in range(2):
        ins = refs[side * NX : (side + 1) * NX]
        for r in range(NX):
            outs[side * NX + r][...] = (ins[0][r] + ins[1][r]) + (ins[2][r] + ins[3][r])


def in_vmem(kernel, args, shape):
    vm = pl.BlockSpec(memory_space=pltpu.VMEM)
    out = pl.pallas_call(
        kernel,
        out_shape=[jax.ShapeDtypeStruct(shape, jnp.float32)] * (2 * NX),
        in_specs=[vm] * len(args),
        out_specs=[vm] * (2 * NX),
        compiler_params=pltpu.CompilerParams(vmem_limit_bytes=16 << 20),
    )(*args)
    return out[:NX], out[NX:]


def local_gram_kernel(*refs):
    gram, image_t = refs[2 * NX :]
    sides = [
        (side[0][...] + side[1][...]) + (side[2][...] + side[3][...])
        for side in (refs[:NX], refs[NX : 2 * NX])
    ]
    image = jnp.concatenate(sides, axis=0)
    image_t[...] = image.T
    gram[...] = lax.dot_general(
        image, image, (((0,), (0,)), ((), ())), precision=HIGH, preferred_element_type=jnp.float32
    )


def local_gram(top, bottom):
    vm = pl.BlockSpec(memory_space=pltpu.VMEM)
    return pl.pallas_call(
        local_gram_kernel,
        out_shape=[
            jax.ShapeDtypeStruct((K, K), jnp.float32),
            jax.ShapeDtypeStruct((K, BS), jnp.float32),
        ],
        in_specs=[vm] * (2 * NX),
        out_specs=[vm, vm],
        compiler_params=pltpu.CompilerParams(vmem_limit_bytes=16 << 20),
        name="local_gram",
    )(*top, *bottom)


def spread(mine, theirs):
    return in_vmem(spread_kernel, (mine, theirs), (NY, BS // 2, K))


def add_up(top, bottom):
    return in_vmem(add_up_kernel, (*top, *bottom), (BS // 2, K))


def factor_block(d):
    groups = [d[8 * g : 8 * g + 8, :] for g in range(8)]
    sub = lax.broadcasted_iota(jnp.int32, (8, 128), 0)
    for p in range(8):
        r = groups[p]
        cols = [jnp.broadcast_to(r[:, 8 * p + k : 8 * p + k + 1], (8, 128)) for k in range(8)]
        a = [
            [jnp.broadcast_to(cols[k][i : i + 1, :], (8, 128)) if i <= k else None for k in range(8)]
            for i in range(8)
        ]
        rs = [None] * 8
        rows = []
        for i in range(8):
            rs[i] = lax.rsqrt(a[i][i])
            for k in range(i + 1, 8):
                a[i][k] = a[i][k] * rs[i]
            for k in range(i + 1, 8):
                for l in range(k, 8):
                    a[k][l] = a[k][l] - a[i][k] * a[i][l]
            row = jnp.broadcast_to(r[i : i + 1, :], (8, 128))
            for k in range(i):
                row = row - a[k][i] * rows[k]
            rows.append(row * rs[i])
        for g in range(p + 1, 8):
            cur = groups[g]
            mult = []
            for i in range(8):
                m = jnp.broadcast_to(cur[:, 8 * p + i : 8 * p + i + 1], (8, 128))
                for k in range(i):
                    m = m - mult[k] * a[k][i]
                mult.append(m * rs[i])
            for i in range(8):
                cur = cur - mult[i] * rows[i]
            groups[g] = cur
        new = rows[0]
        for i in range(1, 8):
            new = jnp.where(sub == i, rows[i], new)
        groups[p] = new
    return jnp.concatenate(groups, axis=0)


def factor_kernel(g_ref, xt_ref, tri_ref, basis_ref, a_ref, w_ref):
    a_ref[...] = g_ref[...]
    w_ref[...] = xt_ref[...]
    lane = lax.broadcasted_iota(jnp.int32, (HB, 128), 1)
    srow = lax.broadcasted_iota(jnp.int32, (HB, 128), 0)
    eye = jnp.where(lane - HB == srow, 1.0, 0.0).astype(jnp.float32)
    low = lane < HB
    rown = lax.broadcasted_iota(jnp.int32, (HB, K), 0)
    coln = lax.broadcasted_iota(jnp.int32, (HB, K), 1)

    def one_block(b, carry):
        lo = pl.multiple_of(b * HB, HB)
        here = a_ref[pl.ds(lo, HB), :]
        tile = jnp.where(b >= 2, here[:, 128:], here[:, :128])
        tile = jnp.where(b % 2 == 1, pltpu.roll(tile, HB, 1), tile)
        res = factor_block(jnp.where(low, tile, eye))
        inv = jnp.where(low, 0.0, res)
        both = jnp.concatenate([here, w_ref[pl.ds(lo, HB), :]], axis=1)
        out = jnp.dot(
            inv,
            jnp.concatenate([jnp.zeros_like(both), both], axis=0),
            precision=HIGH,
            preferred_element_type=jnp.float32,
        )
        upper = jnp.where(coln >= rown + lo, out[:, :K], 0.0)
        tri_ref[pl.ds(lo, HB), :] = upper
        w_ref[pl.ds(lo, HB), :] = out[:, K:]

        @pl.when(b < K // HB - 1)
        def _():
            upd = lax.dot_general(
                jnp.where(coln >= lo + HB, upper, 0.0),
                jnp.concatenate([upper, out[:, K:]], axis=1),
                (((0,), (0,)), ((), ())),
                precision=HIGH,
                preferred_element_type=jnp.float32,
            )
            a_ref[...] = a_ref[...] - upd[:, :K]
            w_ref[...] = w_ref[...] - upd[:, K:]

        return carry

    lax.fori_loop(0, K // HB, one_block, 0)
    basis_ref[...] = w_ref[...].T


def factor(gram, xt):
    vm = pl.BlockSpec(memory_space=pltpu.VMEM)
    return pl.pallas_call(
        factor_kernel,
        out_shape=[
            jax.ShapeDtypeStruct((K, K), jnp.float32),
            jax.ShapeDtypeStruct((BS, K), jnp.float32),
        ],
        in_specs=[vm, vm],
        out_specs=[vm, vm],
        scratch_shapes=[pltpu.VMEM((K, K), jnp.float32), pltpu.VMEM((K, BS), jnp.float32)],
        name="factor",
    )(gram, xt)


def hand_on_kernel(x_ref, o_ref):
    o_ref[...] = x_ref[...]


def hand_on(x):
    vm = pl.BlockSpec(memory_space=pltpu.VMEM)
    return pl.pallas_call(
        hand_on_kernel,
        out_shape=jax.ShapeDtypeStruct(x.shape, x.dtype),
        in_specs=[vm],
        out_specs=vm,
        name="hand_on",
    )(x)


def rank_in_group(group, order):
    n = group.shape[-1]
    key = order * n + jnp.arange(n, dtype=jnp.int32)
    same = group[..., None, :] == group[..., :, None]
    before = key[..., None, :] < key[..., :, None]
    return jnp.sum((same & before).astype(jnp.int32), axis=-1)


def distance_order(d):
    return jnp.where(d == 4, 0, jnp.where(d == 3, 1, jnp.where(d == 5, 2, d + 3)))


def one_device(block_values, block_columns, row_counts, sketch):
    z, x = lax.axis_index("z"), lax.axis_index("x")
    y, core = lax.axis_index("y"), lax.axis_index("core")
    blocks = split(sketch.reshape(BPD, BS, K))
    have = {0: [sketch.reshape(BPD, BS, K)]}
    fwd = {1: [lax.ppermute(blocks[h], "z", ring(NZ, 1)) for h in range(2)]}
    bwd = {1: [lax.ppermute(blocks[h], "z", ring(NZ, -1)) for h in range(2)]}

    slots = BR * S
    live = jnp.arange(S, dtype=jnp.int32)[None, :] < row_counts
    meta = jnp.where(live, block_columns, -1).reshape(slots)
    ids = jnp.arange(slots, dtype=jnp.int32)
    own = meta // BPD
    dist_z = (own // NX - z) % NZ
    dist_x = jnp.where(meta < 0, NX, (own % NX - x) % NX)
    place = dist_x * FULL + rank_in_group(dist_x, distance_order(dist_z))
    spots = jnp.arange(NX * FULL, dtype=jnp.int32)
    wanted = jnp.sum(jnp.where(place[:, None] == spots[None, :], ids[:, None], 0), axis=0)
    wanted = wanted.reshape(NX, FULL)
    flat_values = block_values.reshape(slots, BS, BS)
    metas = [meta.reshape(2, 128)]
    for dx in range(1, NX):
        metas.append(lax.ppermute(metas[0], "x", ring(NX, dx)))
    wanted, metas = lax.optimization_barrier((wanted, metas))
    vals = [*pack(wanted[:1, :FIRST], flat_values), *pack(wanted[1:, :FIRST], flat_values)]
    for dx in range(1, NX):
        vals[dx] = lax.ppermute(vals[dx], "x", ring(NX, dx))

    for step in range(1, 5):
        if step > 1:
            fwd[step] = [None, None]
            bwd[step] = [None, None]
            for h in range(2):
                if step < 4 or h == 0:
                    fwd[step][h] = lax.ppermute(fwd[step - 1][h], "z", ring(NZ, 1))
                if step < 4 or h == 1:
                    bwd[step][h] = lax.ppermute(bwd[step - 1][h], "z", ring(NZ, -1))
        if step < 4:
            have[NZ - step] = fwd[step]
            have[step] = bwd[step]
        else:
            have[4] = [fwd[4][0], bwd[4][1]]

    metas[0] = hand_on(metas[0])
    got = jnp.stack([m.reshape(slots) for m in metas])
    own = got // BPD
    shift = jnp.arange(NX, dtype=jnp.int32)[:, None]
    towards = jnp.where(got < 0, NX, own % NX)
    match = towards == x
    dist = (own // NX - z) % NZ
    place = rank_in_group(towards, distance_order(dist))
    block_row = (ids // S)[None, :]
    group = jnp.where(match, 2 * dist + ((block_row % NC) ^ core), 2 * NZ)
    rank = rank_in_group(group, jnp.zeros_like(group))
    hits = (group[:, :, None] == jnp.arange(2 * NZ)[None, None, :]).astype(jnp.int32)
    counts = jnp.sum(hits, axis=1)
    offsets = jnp.cumsum(counts, axis=0) - counts
    number = jnp.sum(counts, axis=0)
    entry = jnp.sum(hits * offsets[:, None, :], axis=2) + rank
    where = jnp.where(match, group * ENTRIES + entry, -1).reshape(-1)
    row = (NX - shift) % NX * NY + (block_row // NC - y) % NY
    packed = place + 128 * shift + 512 * (got % BPD) + 16384 * row
    filling = 127
    spots = jnp.arange(2 * NZ * ENTRIES, dtype=jnp.int32)
    table = filling + jnp.sum(
        jnp.where(where[:, None] == spots[None, :], packed.reshape(-1)[:, None] - filling, 0),
        axis=0,
    )

    longest = jnp.max(jnp.where(got >= 0, place, -1)) + 1

    def second_part():
        parts = []
        for dx in range(NX):
            sent = flat_values.at[wanted[dx, FIRST:]].get(mode="promise_in_bounds")
            parts.append(lax.ppermute(sent, "x", ring(NX, dx)) if dx else sent)
        return tuple(parts)

    def no_second_part():
        return (jnp.zeros((REST, BS, BS), jnp.bfloat16),) * NX

    more = lax.cond(longest > FIRST, second_part, no_second_part)
    number = jnp.concatenate([number, longest[None]])

    prev = None
    groups = [((0, 1, 7, 2, 6), FULL), ((3, 5), 3 * CAP), ((4,), CAP)]
    for ds, window in groups:
        prev = products(ds, window, table, number, vals, more, [have[d] for d in ds], prev)
    mine, other = prev
    parts = spread(mine, lax.ppermute(other, "core", ring(NC, 1)))
    for axes in (("x", "y"), ("y", "x")):
        moved = [
            [part if r == 0 else lax.ppermute(part, axis, ring(NX, r)) for r, part in enumerate(side)]
            for axis, side in zip(axes, parts)
        ]
        if axes[0] == "x":
            parts = add_up(*moved)
    gram, image_t = local_gram(*moved)
    plane = ("x", "y", "core")
    n_plane = NX * NY * NC
    piece = K // n_plane
    gram = gram.reshape(n_plane, piece, K)
    part = jnp.sum(lax.all_to_all(gram, plane, 0, 0, tiled=True), axis=0)
    part = jnp.broadcast_to(part[None], (NZ, piece, K))
    part = jnp.sum(lax.all_to_all(part, "z", 0, 0, tiled=True), axis=0) / (NZ * n_plane * BS)
    part = jnp.broadcast_to(part[None], (n_plane, piece, K))
    gram = lax.all_to_all(part, plane, 0, 0, tiled=True).reshape(K, K)
    triangle, basis = factor(gram, image_t)
    return basis, triangle


def solution(mesh):
    axes = ("z", "x", "y", "core")
    fine = Mesh(mesh.devices.reshape(NZ, NX, NY, NC), axes)
    rows, cols = ("z", "x"), ("y", "core")
    return jax.shard_map(
        one_device,
        mesh=fine,
        in_specs=(P(rows, cols, None, None), P(rows, cols), P(rows, cols), P(axes, None)),
        out_specs=(P(axes, None), P()),
        check_vma=False,
    )
```

```python
import functools

import jax
import jax.numpy as jnp
from jax import lax
from jax.experimental import pallas as pl
from jax.experimental.pallas import tpu as pltpu
from jax.sharding import Mesh
from jax.sharding import PartitionSpec as P

NZ, NX, NY, NC = 8, 4, 4, 2
CAP = 12
FULL = NZ * CAP
FIRST = 72
REST = FULL - FIRST
BR, S, BS, K = 8, 32, 128, 256
BPD = 32
ENTRIES = NX * CAP
ROWS = NX * BR
HIGH = lax.Precision.HIGHEST


def ring(n, shift):
    return [(i, (i + shift) % n) for i in range(n)]


def split_kernel(x_ref, near, far, buf, isem, osem):
    step = BPD // 4
    loads, stores = [], []
    for c in range(4):
        out = (near, far)[c // 2].at[pl.ds(c % 2 * step, step)]
        loads.append(pltpu.make_async_copy(x_ref.at[pl.ds(c * step, step)], buf.at[c], isem.at[c]))
        stores.append(pltpu.make_async_copy(buf.at[c], out, osem.at[c]))
    for c in loads:
        c.start()
    for load, store in zip(loads, stores):
        load.wait()
        store.start()
    for c in stores:
        c.wait()


def split(blocks):
    half = jax.ShapeDtypeStruct((BPD // 2, BS, K), jnp.bfloat16)
    anyspec = pl.BlockSpec(memory_space=pl.ANY)
    return pl.pallas_call(
        split_kernel,
        out_shape=[half, half],
        in_specs=[anyspec],
        out_specs=[anyspec, anyspec],
        scratch_shapes=[
            pltpu.VMEM((4, BPD // 4, BS, K), jnp.bfloat16),
            pltpu.SemaphoreType.DMA((4,)),
            pltpu.SemaphoreType.DMA((4,)),
        ],
        compiler_params=pltpu.CompilerParams(vmem_limit_bytes=60 << 20),
        cost_estimate=pl.CostEstimate(
            flops=0, bytes_accessed=2 * BPD * BS * K * 2, transcendentals=0
        ),
        name="split",
    )(blocks)


def pack_kernel(n, index, values, *refs):
    outs, (buf, gsem, osem) = refs[:n], refs[n:]
    for m in range(n):

        def fetch(i, carry, m=m):
            pltpu.make_async_copy(
                values.at[index[m * FIRST + i]], buf.at[m, i], gsem.at[m]
            ).start()
            return carry

        lax.fori_loop(0, FIRST, fetch, 0, unroll=8)
    stores = []
    for m in range(n):
        pltpu.make_async_copy(values.at[pl.ds(0, FIRST)], buf.at[m], gsem.at[m]).wait()
        stores.append(pltpu.make_async_copy(buf.at[m], outs[m], osem.at[m]))
        stores[-1].start()
    for c in stores:
        c.wait()


def pack(index, values):
    n = index.shape[0]
    anyspec = pl.BlockSpec(memory_space=pl.ANY)
    return pl.pallas_call(
        functools.partial(pack_kernel, n),
        out_shape=[jax.ShapeDtypeStruct((FIRST, BS, BS), jnp.bfloat16)] * n,
        grid_spec=pltpu.PrefetchScalarGridSpec(
            num_scalar_prefetch=1,
            grid=(1,),
            in_specs=[anyspec],
            out_specs=[anyspec] * n,
            scratch_shapes=[
                pltpu.VMEM((n, FIRST, BS, BS), jnp.bfloat16),
                pltpu.SemaphoreType.DMA((n,)),
                pltpu.SemaphoreType.DMA((n,)),
            ],
        ),
        compiler_params=pltpu.CompilerParams(vmem_limit_bytes=16 << 20),
        cost_estimate=pl.CostEstimate(
            flops=0, bytes_accessed=2 * n * FIRST * BS * BS * 2, transcendentals=0
        ),
    )(index.reshape(-1), values)


def products_kernel(ds, halves, window, first, *refs):
    refs = list(refs)
    tbl, num = refs[0], refs[1]
    whole = window == FULL
    vals = refs[2 : 2 + NX]
    pos = 2 + NX
    if whole:
        more = refs[pos : pos + NX]
        pos += NX
    tabs = []
    for h in halves:
        tabs.append(refs[pos : pos + h])
        pos += h
    if not first:
        pos += 2
    rows = refs[pos : pos + 2]
    vb, tb, vsem, tsem, msem = refs[pos + 2 :]
    size = min(window, FIRST)
    loads = [
        pltpu.make_async_copy(
            vals[dx].at[pl.ds(0, size)], vb.at[dx, pl.ds(0, size)], vsem.at[dx]
        )
        for dx in range(NX)
    ]
    for i in range(len(ds)):
        part = BPD // halves[i]
        loads += [
            pltpu.make_async_copy(tabs[i][h], tb.at[i, pl.ds(h * part, part)], tsem.at[i, h])
            for h in range(halves[i])
        ]
    for c in loads:
        c.start()
    vb[0, window] = jnp.zeros((BS, BS), jnp.bfloat16)
    for h in range(2):
        if first:
            rows[h][...] = jnp.zeros_like(rows[h])
    if whole:

        @pl.when(num[2 * NZ] > FIRST)
        def _():
            for dx in range(NX):
                c = pltpu.make_async_copy(more[dx], vb.at[dx, pl.ds(FIRST, REST)], msem)
                c.start()
                c.wait()

    for c in loads:
        c.wait()

    def one_distance(i, carry):
        d = ds[0]
        for k in range(1, len(ds)):
            d = jnp.where(i == k, ds[k], d)
        for h in range(2):
            which = 2 * d + h

            def step(j, carry, h=h, which=which):
                for u in range(4):
                    entry = tbl[which * ENTRIES + j * 4 + u]
                    p = jnp.minimum(jnp.bitwise_and(entry, 127), window)
                    dx = jnp.bitwise_and(lax.shift_right_logical(entry, 7), 3)
                    t = jnp.bitwise_and(lax.shift_right_logical(entry, 9), 31)
                    row = lax.shift_right_logical(entry, 14)
                    rows[h][row] += jnp.dot(
                        vb[dx, p], tb[i, t], preferred_element_type=jnp.float32
                    )
                return carry

            lax.fori_loop(0, (num[which] + 3) // 4, step, 0)
        return carry

    lax.fori_loop(0, len(ds), one_distance, 0)


def products(ds, window, tbl, num, vals, more, tabs, prev):
    halves = tuple(len(t) for t in tabs)
    first = prev is None
    args = list(vals) + (list(more) if window == FULL else [])
    args += [a for t in tabs for a in t]
    smem = pl.BlockSpec(memory_space=pltpu.SMEM)
    vmem = pl.BlockSpec(memory_space=pltpu.VMEM)
    anyspec = pl.BlockSpec(memory_space=pl.ANY)
    specs = [smem, smem] + [anyspec] * len(args)
    aliases = {}
    if not first:
        aliases = {len(specs): 0, len(specs) + 1: 1}
        args += list(prev)
        specs += [vmem, vmem]
    nd = len(ds)
    return pl.pallas_call(
        functools.partial(products_kernel, ds, halves, window, first),
        out_shape=[jax.ShapeDtypeStruct((ROWS // 2, BS, K), jnp.float32)] * 2,
        in_specs=specs,
        out_specs=[vmem, vmem],
        scratch_shapes=[
            pltpu.VMEM((NX, window + 1, BS, BS), jnp.bfloat16),
            pltpu.VMEM((nd, BPD, BS, K), jnp.bfloat16),
            pltpu.SemaphoreType.DMA((NX,)),
            pltpu.SemaphoreType.DMA((nd, 2)),
            pltpu.SemaphoreType.DMA,
        ],
        input_output_aliases=aliases,
        compiler_params=pltpu.CompilerParams(vmem_limit_bytes=40 << 20),
        cost_estimate=pl.CostEstimate(
            flops=nd * 20 * 2 * BS * BS * K,
            bytes_accessed=nd * BPD * BS * K * 2 + NX * window * BS * BS * 2,
            transcendentals=0,
        ),
    )(tbl, num, *args)


HB = 64


def spread_kernel(mine, theirs, *outs):
    top, bottom = outs[:NX], outs[NX:]
    half = BS // 2
    for r in range(NX):

        def step(j, carry, r=r):
            i = NY * r + j
            top[r][j] = mine[i, :half] + theirs[i, :half]
            i = NY * j + r
            bottom[r][j] = mine[i, half:] + theirs[i, half:]
            return carry

        lax.fori_loop(0, NX, step, 0)


def add_up_kernel(*refs):
    outs = refs[2 * NX :]
    for side in range(2):
        ins = refs[side : 2 * NX : 2]
        for r in range(NX):
            outs[side * NX + r][...] = (ins[0][r] + ins[1][r]) + (ins[2][r] + ins[3][r])


def in_vmem(kernel, args, shape):
    vm = pl.BlockSpec(memory_space=pltpu.VMEM)
    out = pl.pallas_call(
        kernel,
        out_shape=[jax.ShapeDtypeStruct(shape, jnp.float32)] * (2 * NX),
        in_specs=[vm] * len(args),
        out_specs=[vm] * (2 * NX),
        compiler_params=pltpu.CompilerParams(vmem_limit_bytes=16 << 20),
    )(*args)
    return out[:NX], out[NX:]


def in_turn(top, bottom):
    return [side[r] for r in (2, 1, 3, 0) for side in (top, bottom)]


def local_gram_kernel(*refs):
    gram, image_t = refs[2 * NX :]
    sides = [
        (side[0][...] + side[1][...]) + (side[2][...] + side[3][...])
        for side in (refs[: 2 * NX : 2], refs[1 : 2 * NX : 2])
    ]
    image = jnp.concatenate(sides, axis=0)
    image_t[...] = image.T
    gram[...] = lax.dot_general(
        image, image, (((0,), (0,)), ((), ())), precision=HIGH, preferred_element_type=jnp.float32
    )


def local_gram(top, bottom):
    vm = pl.BlockSpec(memory_space=pltpu.VMEM)
    return pl.pallas_call(
        local_gram_kernel,
        out_shape=[
            jax.ShapeDtypeStruct((K, K), jnp.float32),
            jax.ShapeDtypeStruct((K, BS), jnp.float32),
        ],
        in_specs=[vm] * (2 * NX),
        out_specs=[vm, vm],
        compiler_params=pltpu.CompilerParams(vmem_limit_bytes=16 << 20),
        name="local_gram",
    )(*in_turn(top, bottom))


def spread(mine, theirs):
    return in_vmem(spread_kernel, (mine, theirs), (NY, BS // 2, K))


def add_up(top, bottom):
    return in_vmem(add_up_kernel, in_turn(top, bottom), (BS // 2, K))


def factor_block(d):
    groups = [d[8 * g : 8 * g + 8, :] for g in range(8)]
    sub = lax.broadcasted_iota(jnp.int32, (8, 128), 0)
    for p in range(8):
        r = groups[p]
        cols = [jnp.broadcast_to(r[:, 8 * p + k : 8 * p + k + 1], (8, 128)) for k in range(8)]
        a = [
            [jnp.broadcast_to(cols[k][i : i + 1, :], (8, 128)) if i <= k else None for k in range(8)]
            for i in range(8)
        ]
        rs = [None] * 8
        rows = []
        for i in range(8):
            rs[i] = lax.rsqrt(a[i][i])
            for k in range(i + 1, 8):
                a[i][k] = a[i][k] * rs[i]
            for k in range(i + 1, 8):
                for l in range(k, 8):
                    a[k][l] = a[k][l] - a[i][k] * a[i][l]
            row = jnp.broadcast_to(r[i : i + 1, :], (8, 128))
            for k in range(i):
                row = row - a[k][i] * rows[k]
            rows.append(row * rs[i])
        for g in range(p + 1, 8):
            cur = groups[g]
            mult = []
            for i in range(8):
                m = jnp.broadcast_to(cur[:, 8 * p + i : 8 * p + i + 1], (8, 128))
                for k in range(i):
                    m = m - mult[k] * a[k][i]
                mult.append(m * rs[i])
            for i in range(8):
                cur = cur - mult[i] * rows[i]
            groups[g] = cur
        new = rows[0]
        for i in range(1, 8):
            new = jnp.where(sub == i, rows[i], new)
        groups[p] = new
    return jnp.concatenate(groups, axis=0)


def factor_kernel(g_ref, xt_ref, tri_ref, basis_ref, a_ref, w_ref):
    a_ref[...] = g_ref[...]
    w_ref[...] = xt_ref[...]
    lane = lax.broadcasted_iota(jnp.int32, (HB, 128), 1)
    srow = lax.broadcasted_iota(jnp.int32, (HB, 128), 0)
    eye = jnp.where(lane - HB == srow, 1.0, 0.0).astype(jnp.float32)
    low = lane < HB
    rown = lax.broadcasted_iota(jnp.int32, (HB, K), 0)
    coln = lax.broadcasted_iota(jnp.int32, (HB, K), 1)

    def one_block(b, carry):
        lo = pl.multiple_of(b * HB, HB)
        here = a_ref[pl.ds(lo, HB), :]
        tile = jnp.where(b >= 2, here[:, 128:], here[:, :128])
        tile = jnp.where(b % 2 == 1, pltpu.roll(tile, HB, 1), tile)
        res = factor_block(jnp.where(low, tile, eye))
        inv = jnp.where(low, 0.0, res)
        both = jnp.concatenate([here, w_ref[pl.ds(lo, HB), :]], axis=1)
        out = jnp.dot(
            inv,
            jnp.concatenate([jnp.zeros_like(both), both], axis=0),
            precision=HIGH,
            preferred_element_type=jnp.float32,
        )
        upper = jnp.where(coln >= rown + lo, out[:, :K], 0.0)
        tri_ref[pl.ds(lo, HB), :] = upper
        w_ref[pl.ds(lo, HB), :] = out[:, K:]

        @pl.when(b < K // HB - 1)
        def _():
            upd = lax.dot_general(
                jnp.where(coln >= lo + HB, upper, 0.0),
                jnp.concatenate([upper, out[:, K:]], axis=1),
                (((0,), (0,)), ((), ())),
                precision=HIGH,
                preferred_element_type=jnp.float32,
            )
            a_ref[...] = a_ref[...] - upd[:, :K]
            w_ref[...] = w_ref[...] - upd[:, K:]

        return carry

    lax.fori_loop(0, K // HB, one_block, 0)
    basis_ref[...] = w_ref[...].T


def factor(gram, xt):
    vm = pl.BlockSpec(memory_space=pltpu.VMEM)
    return pl.pallas_call(
        factor_kernel,
        out_shape=[
            jax.ShapeDtypeStruct((K, K), jnp.float32),
            jax.ShapeDtypeStruct((BS, K), jnp.float32),
        ],
        in_specs=[vm, vm],
        out_specs=[vm, vm],
        scratch_shapes=[pltpu.VMEM((K, K), jnp.float32), pltpu.VMEM((K, BS), jnp.float32)],
        name="factor",
    )(gram, xt)


def hand_on_kernel(x_ref, o_ref):
    o_ref[...] = x_ref[...]


def hand_on(x):
    vm = pl.BlockSpec(memory_space=pltpu.VMEM)
    return pl.pallas_call(
        hand_on_kernel,
        out_shape=jax.ShapeDtypeStruct(x.shape, x.dtype),
        in_specs=[vm],
        out_specs=vm,
        name="hand_on",
    )(x)


def rank_in_group(group, order):
    n = group.shape[-1]
    key = order * n + jnp.arange(n, dtype=jnp.int32)
    same = group[..., None, :] == group[..., :, None]
    before = key[..., None, :] < key[..., :, None]
    return jnp.sum((same & before).astype(jnp.int32), axis=-1)


def distance_order(d):
    return jnp.where(d == 4, 0, jnp.where(d == 3, 1, jnp.where(d == 5, 2, d + 3)))


def one_device(block_values, block_columns, row_counts, sketch):
    z, x = lax.axis_index("z"), lax.axis_index("x")
    y, core = lax.axis_index("y"), lax.axis_index("core")
    blocks = split(sketch.reshape(BPD, BS, K))
    have = {0: [sketch.reshape(BPD, BS, K)]}
    fwd = {1: [lax.ppermute(blocks[h], "z", ring(NZ, 1)) for h in range(2)]}
    bwd = {1: [lax.ppermute(blocks[h], "z", ring(NZ, -1)) for h in range(2)]}

    slots = BR * S
    live = jnp.arange(S, dtype=jnp.int32)[None, :] < row_counts
    meta = jnp.where(live, block_columns, -1).reshape(slots)
    ids = jnp.arange(slots, dtype=jnp.int32)
    own = meta // BPD
    dist_z = (own // NX - z) % NZ
    dist_x = jnp.where(meta < 0, NX, (own % NX - x) % NX)
    place = dist_x * FULL + rank_in_group(dist_x, distance_order(dist_z))
    spots = jnp.arange(NX * FULL, dtype=jnp.int32)
    wanted = jnp.sum(jnp.where(place[:, None] == spots[None, :], ids[:, None], 0), axis=0)
    wanted = wanted.reshape(NX, FULL)
    flat_values = block_values.reshape(slots, BS, BS)
    metas = [meta.reshape(2, 128)]
    for dx in range(1, NX):
        metas.append(lax.ppermute(metas[0], "x", ring(NX, dx)))
    wanted, metas = lax.optimization_barrier((wanted, metas))
    vals = [*pack(wanted[:1, :FIRST], flat_values), *pack(wanted[1:, :FIRST], flat_values)]
    for dx in range(1, NX):
        vals[dx] = lax.ppermute(vals[dx], "x", ring(NX, dx))

    for step in range(1, 5):
        if step > 1:
            fwd[step] = [None, None]
            bwd[step] = [None, None]
            for h in range(2):
                if step < 4 or h == 0:
                    fwd[step][h] = lax.ppermute(fwd[step - 1][h], "z", ring(NZ, 1))
                if step < 4 or h == 1:
                    bwd[step][h] = lax.ppermute(bwd[step - 1][h], "z", ring(NZ, -1))
        if step < 4:
            have[NZ - step] = fwd[step]
            have[step] = bwd[step]
        else:
            have[4] = [fwd[4][0], bwd[4][1]]

    metas[0] = hand_on(metas[0])
    got = jnp.stack([m.reshape(slots) for m in metas])
    own = got // BPD
    shift = jnp.arange(NX, dtype=jnp.int32)[:, None]
    towards = jnp.where(got < 0, NX, own % NX)
    match = towards == x
    dist = (own // NX - z) % NZ
    place = rank_in_group(towards, distance_order(dist))
    block_row = (ids // S)[None, :]
    group = jnp.where(match, 2 * dist + ((block_row % NC) ^ core), 2 * NZ)
    rank = rank_in_group(group, jnp.zeros_like(group))
    hits = (group[:, :, None] == jnp.arange(2 * NZ)[None, None, :]).astype(jnp.int32)
    counts = jnp.sum(hits, axis=1)
    offsets = jnp.cumsum(counts, axis=0) - counts
    number = jnp.sum(counts, axis=0)
    entry = jnp.sum(hits * offsets[:, None, :], axis=2) + rank
    where = jnp.where(match, group * ENTRIES + entry, -1).reshape(-1)
    row = (NX - shift) % NX * NY + (block_row // NC - y) % NY
    packed = place + 128 * shift + 512 * (got % BPD) + 16384 * row
    filling = 127
    spots = jnp.arange(2 * NZ * ENTRIES, dtype=jnp.int32)
    table = filling + jnp.sum(
        jnp.where(where[:, None] == spots[None, :], packed.reshape(-1)[:, None] - filling, 0),
        axis=0,
    )

    longest = jnp.max(jnp.where(got >= 0, place, -1)) + 1

    def second_part():
        parts = []
        for dx in range(NX):
            sent = flat_values.at[wanted[dx, FIRST:]].get(mode="promise_in_bounds")
            parts.append(lax.ppermute(sent, "x", ring(NX, dx)) if dx else sent)
        return tuple(parts)

    def no_second_part():
        return (jnp.zeros((REST, BS, BS), jnp.bfloat16),) * NX

    more = lax.cond(longest > FIRST, second_part, no_second_part)
    number = jnp.concatenate([number, longest[None]])

    prev = None
    groups = [((0, 1, 7, 2, 6), FULL), ((3, 5), 3 * CAP), ((4,), CAP)]
    for ds, window in groups:
        prev = products(ds, window, table, number, vals, more, [have[d] for d in ds], prev)
    mine, other = prev
    parts = spread(mine, lax.ppermute(other, "core", ring(NC, 1)))
    for axes in (("x", "y"), ("y", "x")):
        moved = [list(side) for side in parts]
        for r in (2, 1, 3):
            for axis, side in zip(axes, moved):
                side[r] = lax.ppermute(side[r], axis, ring(NX, r))
        if axes[0] == "x":
            parts = add_up(*moved)
    gram, image_t = local_gram(*moved)
    plane = ("x", "y", "core")
    n_plane = NX * NY * NC
    piece = K // n_plane
    gram = gram.reshape(n_plane, piece, K)
    part = jnp.sum(lax.all_to_all(gram, plane, 0, 0, tiled=True), axis=0)
    part = jnp.broadcast_to(part[None], (NZ, piece, K))
    part = jnp.sum(lax.all_to_all(part, "z", 0, 0, tiled=True), axis=0) / (NZ * n_plane * BS)
    part = jnp.broadcast_to(part[None], (n_plane, piece, K))
    gram = lax.all_to_all(part, plane, 0, 0, tiled=True).reshape(K, K)
    triangle, basis = factor(gram, image_t)
    return basis, triangle


def solution(mesh):
    axes = ("z", "x", "y", "core")
    fine = Mesh(mesh.devices.reshape(NZ, NX, NY, NC), axes)
    rows, cols = ("z", "x"), ("y", "core")
    return jax.shard_map(
        one_device,
        mesh=fine,
        in_specs=(P(rows, cols, None, None), P(rows, cols), P(rows, cols), P(axes, None)),
        out_specs=(P(axes, None), P()),
        check_vma=False,
    )
```

```python
import functools

import jax
import jax.numpy as jnp
from jax import lax
from jax.experimental import pallas as pl
from jax.experimental.pallas import tpu as pltpu
from jax.sharding import Mesh
from jax.sharding import PartitionSpec as P

NZ, NX, NY, NC = 8, 4, 4, 2
CAP = 12
FULL = NZ * CAP
FIRST = 72
REST = FULL - FIRST
BR, S, BS, K = 8, 32, 128, 256
BPD = 32
ENTRIES = NX * CAP
ROWS = NX * BR
HIGH = lax.Precision.HIGHEST


def ring(n, shift):
    return [(i, (i + shift) % n) for i in range(n)]


def split_kernel(x_ref, near, far, buf, isem, osem):
    step = BPD // 4
    loads, stores = [], []
    for c in range(4):
        out = (near, far)[c // 2].at[pl.ds(c % 2 * step, step)]
        loads.append(pltpu.make_async_copy(x_ref.at[pl.ds(c * step, step)], buf.at[c], isem.at[c]))
        stores.append(pltpu.make_async_copy(buf.at[c], out, osem.at[c]))
    for c in loads:
        c.start()
    for load, store in zip(loads, stores):
        load.wait()
        store.start()
    for c in stores:
        c.wait()


def split(blocks):
    half = jax.ShapeDtypeStruct((BPD // 2, BS, K), jnp.bfloat16)
    anyspec = pl.BlockSpec(memory_space=pl.ANY)
    return pl.pallas_call(
        split_kernel,
        out_shape=[half, half],
        in_specs=[anyspec],
        out_specs=[anyspec, anyspec],
        scratch_shapes=[
            pltpu.VMEM((4, BPD // 4, BS, K), jnp.bfloat16),
            pltpu.SemaphoreType.DMA((4,)),
            pltpu.SemaphoreType.DMA((4,)),
        ],
        compiler_params=pltpu.CompilerParams(vmem_limit_bytes=60 << 20),
        cost_estimate=pl.CostEstimate(
            flops=0, bytes_accessed=2 * BPD * BS * K * 2, transcendentals=0
        ),
        name="split",
    )(blocks)


def pack_kernel(n, index, values, *refs):
    outs, (buf, gsem, osem) = refs[:n], refs[n:]
    for m in range(n):

        def fetch(i, carry, m=m):
            pltpu.make_async_copy(
                values.at[index[m * FIRST + i]], buf.at[m, i], gsem.at[m]
            ).start()
            return carry

        lax.fori_loop(0, FIRST, fetch, 0, unroll=8)
    stores = []
    for m in range(n):
        pltpu.make_async_copy(values.at[pl.ds(0, FIRST)], buf.at[m], gsem.at[m]).wait()
        stores.append(pltpu.make_async_copy(buf.at[m], outs[m], osem.at[m]))
        stores[-1].start()
    for c in stores:
        c.wait()


def pack(index, values):
    n = index.shape[0]
    anyspec = pl.BlockSpec(memory_space=pl.ANY)
    return pl.pallas_call(
        functools.partial(pack_kernel, n),
        out_shape=[jax.ShapeDtypeStruct((FIRST, BS, BS), jnp.bfloat16)] * n,
        grid_spec=pltpu.PrefetchScalarGridSpec(
            num_scalar_prefetch=1,
            grid=(1,),
            in_specs=[anyspec],
            out_specs=[anyspec] * n,
            scratch_shapes=[
                pltpu.VMEM((n, FIRST, BS, BS), jnp.bfloat16),
                pltpu.SemaphoreType.DMA((n,)),
                pltpu.SemaphoreType.DMA((n,)),
            ],
        ),
        compiler_params=pltpu.CompilerParams(vmem_limit_bytes=16 << 20),
        cost_estimate=pl.CostEstimate(
            flops=0, bytes_accessed=2 * n * FIRST * BS * BS * 2, transcendentals=0
        ),
    )(index.reshape(-1), values)


def products_kernel(ds, halves, window, first, *refs):
    refs = list(refs)
    tbl, num = refs[0], refs[1]
    whole = window == FULL
    vals = refs[2 : 2 + NX]
    pos = 2 + NX
    if whole:
        more = refs[pos : pos + NX]
        pos += NX
    tabs = []
    for h in halves:
        tabs.append(refs[pos : pos + h])
        pos += h
    if not first:
        pos += 2
    rows = refs[pos : pos + 2]
    vb, tb, vsem, tsem, msem = refs[pos + 2 :]
    size = min(window, FIRST)
    loads = [
        pltpu.make_async_copy(
            vals[dx].at[pl.ds(0, size)], vb.at[dx, pl.ds(0, size)], vsem.at[dx]
        )
        for dx in range(NX)
    ]
    for i in range(len(ds)):
        part = BPD // halves[i]
        loads += [
            pltpu.make_async_copy(tabs[i][h], tb.at[i, pl.ds(h * part, part)], tsem.at[i, h])
            for h in range(halves[i])
        ]
    for c in loads:
        c.start()
    vb[0, window] = jnp.zeros((BS, BS), jnp.bfloat16)
    for h in range(2):
        if first:
            rows[h][...] = jnp.zeros_like(rows[h])
    if whole:

        @pl.when(num[2 * NZ] > FIRST)
        def _():
            for dx in range(NX):
                c = pltpu.make_async_copy(more[dx], vb.at[dx, pl.ds(FIRST, REST)], msem)
                c.start()
                c.wait()

    for c in loads:
        c.wait()

    def one_distance(i, carry):
        d = ds[0]
        for k in range(1, len(ds)):
            d = jnp.where(i == k, ds[k], d)
        for h in range(2):
            which = 2 * d + h

            def step(j, carry, h=h, which=which):
                for u in range(4):
                    entry = tbl[which * ENTRIES + j * 4 + u]
                    p = jnp.minimum(jnp.bitwise_and(entry, 127), window)
                    dx = jnp.bitwise_and(lax.shift_right_logical(entry, 7), 3)
                    t = jnp.bitwise_and(lax.shift_right_logical(entry, 9), 31)
                    row = lax.shift_right_logical(entry, 14)
                    rows[h][row] += jnp.dot(
                        vb[dx, p], tb[i, t], preferred_element_type=jnp.float32
                    )
                return carry

            lax.fori_loop(0, (num[which] + 3) // 4, step, 0)
        return carry

    lax.fori_loop(0, len(ds), one_distance, 0)


def products(ds, window, tbl, num, vals, more, tabs, prev):
    halves = tuple(len(t) for t in tabs)
    first = prev is None
    args = list(vals) + (list(more) if window == FULL else [])
    args += [a for t in tabs for a in t]
    smem = pl.BlockSpec(memory_space=pltpu.SMEM)
    vmem = pl.BlockSpec(memory_space=pltpu.VMEM)
    anyspec = pl.BlockSpec(memory_space=pl.ANY)
    specs = [smem, smem] + [anyspec] * len(args)
    aliases = {}
    if not first:
        aliases = {len(specs): 0, len(specs) + 1: 1}
        args += list(prev)
        specs += [vmem, vmem]
    nd = len(ds)
    return pl.pallas_call(
        functools.partial(products_kernel, ds, halves, window, first),
        out_shape=[jax.ShapeDtypeStruct((ROWS // 2, BS, K), jnp.float32)] * 2,
        in_specs=specs,
        out_specs=[vmem, vmem],
        scratch_shapes=[
            pltpu.VMEM((NX, window + 1, BS, BS), jnp.bfloat16),
            pltpu.VMEM((nd, BPD, BS, K), jnp.bfloat16),
            pltpu.SemaphoreType.DMA((NX,)),
            pltpu.SemaphoreType.DMA((nd, 2)),
            pltpu.SemaphoreType.DMA,
        ],
        input_output_aliases=aliases,
        compiler_params=pltpu.CompilerParams(vmem_limit_bytes=40 << 20),
        cost_estimate=pl.CostEstimate(
            flops=nd * 20 * 2 * BS * BS * K,
            bytes_accessed=nd * BPD * BS * K * 2 + NX * window * BS * BS * 2,
            transcendentals=0,
        ),
    )(tbl, num, *args)


HB = 64


def spread_kernel(mine, theirs, *outs):
    top, bottom = outs[:NX], outs[NX:]
    half = BS // 2
    for r in range(NX):

        def step(j, carry, r=r):
            i = NY * r + j
            top[r][j] = mine[i, :half] + theirs[i, :half]
            i = NY * j + r
            bottom[r][j] = mine[i, half:] + theirs[i, half:]
            return carry

        lax.fori_loop(0, NX, step, 0)


def add_up_kernel(*refs):
    ins, outs = refs[:NX], refs[NX:]
    for r in range(NX):
        outs[r][...] = (ins[0][r] + ins[1][r]) + (ins[2][r] + ins[3][r])


def in_vmem(kernel, args, shape, n):
    vm = pl.BlockSpec(memory_space=pltpu.VMEM)
    out = pl.pallas_call(
        kernel,
        out_shape=[jax.ShapeDtypeStruct(shape, jnp.float32)] * n,
        in_specs=[vm] * len(args),
        out_specs=[vm] * n,
        compiler_params=pltpu.CompilerParams(vmem_limit_bytes=16 << 20),
    )(*args)
    return out


def in_turn(top, bottom):
    return [side[r] for r in (2, 1, 3, 0) for side in (top, bottom)]


def local_gram_kernel(*refs):
    gram, image_t = refs[2 * NX :]
    sides = [
        (side[0][...] + side[1][...]) + (side[2][...] + side[3][...])
        for side in (refs[: 2 * NX : 2], refs[1 : 2 * NX : 2])
    ]
    image = jnp.concatenate(sides, axis=0)
    image_t[...] = image.T
    gram[...] = lax.dot_general(
        image, image, (((0,), (0,)), ((), ())), precision=HIGH, preferred_element_type=jnp.float32
    )


def local_gram(top, bottom):
    vm = pl.BlockSpec(memory_space=pltpu.VMEM)
    return pl.pallas_call(
        local_gram_kernel,
        out_shape=[
            jax.ShapeDtypeStruct((K, K), jnp.float32),
            jax.ShapeDtypeStruct((K, BS), jnp.float32),
        ],
        in_specs=[vm] * (2 * NX),
        out_specs=[vm, vm],
        compiler_params=pltpu.CompilerParams(vmem_limit_bytes=16 << 20),
        name="local_gram",
    )(*in_turn(top, bottom))


def spread(mine, theirs):
    out = in_vmem(spread_kernel, (mine, theirs), (NY, BS // 2, K), 2 * NX)
    return out[:NX], out[NX:]


def add_up(side):
    return in_vmem(add_up_kernel, [side[r] for r in (2, 1, 3, 0)], (BS // 2, K), NX)


def factor_block(d):
    groups = [d[8 * g : 8 * g + 8, :] for g in range(8)]
    sub = lax.broadcasted_iota(jnp.int32, (8, 128), 0)
    for p in range(8):
        r = groups[p]
        cols = [jnp.broadcast_to(r[:, 8 * p + k : 8 * p + k + 1], (8, 128)) for k in range(8)]
        a = [
            [jnp.broadcast_to(cols[k][i : i + 1, :], (8, 128)) if i <= k else None for k in range(8)]
            for i in range(8)
        ]
        rs = [None] * 8
        rows = []
        for i in range(8):
            rs[i] = lax.rsqrt(a[i][i])
            for k in range(i + 1, 8):
                a[i][k] = a[i][k] * rs[i]
            for k in range(i + 1, 8):
                for l in range(k, 8):
                    a[k][l] = a[k][l] - a[i][k] * a[i][l]
            row = jnp.broadcast_to(r[i : i + 1, :], (8, 128))
            for k in range(i):
                row = row - a[k][i] * rows[k]
            rows.append(row * rs[i])
        for g in range(p + 1, 8):
            cur = groups[g]
            mult = []
            for i in range(8):
                m = jnp.broadcast_to(cur[:, 8 * p + i : 8 * p + i + 1], (8, 128))
                for k in range(i):
                    m = m - mult[k] * a[k][i]
                mult.append(m * rs[i])
            for i in range(8):
                cur = cur - mult[i] * rows[i]
            groups[g] = cur
        new = rows[0]
        for i in range(1, 8):
            new = jnp.where(sub == i, rows[i], new)
        groups[p] = new
    return jnp.concatenate(groups, axis=0)


def factor_kernel(g_ref, xt_ref, tri_ref, basis_ref, a_ref, w_ref):
    a_ref[...] = g_ref[...]
    w_ref[...] = xt_ref[...]
    lane = lax.broadcasted_iota(jnp.int32, (HB, 128), 1)
    srow = lax.broadcasted_iota(jnp.int32, (HB, 128), 0)
    eye = jnp.where(lane - HB == srow, 1.0, 0.0).astype(jnp.float32)
    low = lane < HB
    rown = lax.broadcasted_iota(jnp.int32, (HB, K), 0)
    coln = lax.broadcasted_iota(jnp.int32, (HB, K), 1)

    def one_block(b, carry):
        lo = pl.multiple_of(b * HB, HB)
        here = a_ref[pl.ds(lo, HB), :]
        tile = jnp.where(b >= 2, here[:, 128:], here[:, :128])
        tile = jnp.where(b % 2 == 1, pltpu.roll(tile, HB, 1), tile)
        res = factor_block(jnp.where(low, tile, eye))
        inv = jnp.where(low, 0.0, res)
        both = jnp.concatenate([here, w_ref[pl.ds(lo, HB), :]], axis=1)
        out = jnp.dot(
            inv,
            jnp.concatenate([jnp.zeros_like(both), both], axis=0),
            precision=HIGH,
            preferred_element_type=jnp.float32,
        )
        upper = jnp.where(coln >= rown + lo, out[:, :K], 0.0)
        tri_ref[pl.ds(lo, HB), :] = upper
        w_ref[pl.ds(lo, HB), :] = out[:, K:]

        @pl.when(b < K // HB - 1)
        def _():
            upd = lax.dot_general(
                jnp.where(coln >= lo + HB, upper, 0.0),
                jnp.concatenate([upper, out[:, K:]], axis=1),
                (((0,), (0,)), ((), ())),
                precision=HIGH,
                preferred_element_type=jnp.float32,
            )
            a_ref[...] = a_ref[...] - upd[:, :K]
            w_ref[...] = w_ref[...] - upd[:, K:]

        return carry

    lax.fori_loop(0, K // HB, one_block, 0)
    basis_ref[...] = w_ref[...].T


def factor(gram, xt):
    vm = pl.BlockSpec(memory_space=pltpu.VMEM)
    return pl.pallas_call(
        factor_kernel,
        out_shape=[
            jax.ShapeDtypeStruct((K, K), jnp.float32),
            jax.ShapeDtypeStruct((BS, K), jnp.float32),
        ],
        in_specs=[vm, vm],
        out_specs=[vm, vm],
        scratch_shapes=[pltpu.VMEM((K, K), jnp.float32), pltpu.VMEM((K, BS), jnp.float32)],
        name="factor",
    )(gram, xt)


def hand_on_kernel(x_ref, o_ref):
    o_ref[...] = x_ref[...]


def hand_on(x):
    vm = pl.BlockSpec(memory_space=pltpu.VMEM)
    return pl.pallas_call(
        hand_on_kernel,
        out_shape=jax.ShapeDtypeStruct(x.shape, x.dtype),
        in_specs=[vm],
        out_specs=vm,
        name="hand_on",
    )(x)


def rank_in_group(group, order):
    n = group.shape[-1]
    key = order * n + jnp.arange(n, dtype=jnp.int32)
    same = group[..., None, :] == group[..., :, None]
    before = key[..., None, :] < key[..., :, None]
    return jnp.sum((same & before).astype(jnp.int32), axis=-1)


def distance_order(d):
    return jnp.where(d == 4, 0, jnp.where(d == 3, 1, jnp.where(d == 5, 2, d + 3)))


def one_device(block_values, block_columns, row_counts, sketch):
    z, x = lax.axis_index("z"), lax.axis_index("x")
    y, core = lax.axis_index("y"), lax.axis_index("core")
    blocks = split(sketch.reshape(BPD, BS, K))
    have = {0: [sketch.reshape(BPD, BS, K)]}
    fwd = {1: [lax.ppermute(blocks[h], "z", ring(NZ, 1)) for h in range(2)]}
    bwd = {1: [lax.ppermute(blocks[h], "z", ring(NZ, -1)) for h in range(2)]}

    slots = BR * S
    live = jnp.arange(S, dtype=jnp.int32)[None, :] < row_counts
    meta = jnp.where(live, block_columns, -1).reshape(slots)
    ids = jnp.arange(slots, dtype=jnp.int32)
    own = meta // BPD
    dist_z = (own // NX - z) % NZ
    dist_x = jnp.where(meta < 0, NX, (own % NX - x) % NX)
    place = dist_x * FULL + rank_in_group(dist_x, distance_order(dist_z))
    spots = jnp.arange(NX * FULL, dtype=jnp.int32)
    wanted = jnp.sum(jnp.where(place[:, None] == spots[None, :], ids[:, None], 0), axis=0)
    wanted = wanted.reshape(NX, FULL)
    flat_values = block_values.reshape(slots, BS, BS)
    metas = [meta.reshape(2, 128)]
    for dx in range(1, NX):
        metas.append(lax.ppermute(metas[0], "x", ring(NX, dx)))
    wanted, metas = lax.optimization_barrier((wanted, metas))
    vals = [*pack(wanted[:1, :FIRST], flat_values), *pack(wanted[1:, :FIRST], flat_values)]
    for dx in range(1, NX):
        vals[dx] = lax.ppermute(vals[dx], "x", ring(NX, dx))

    for step in range(1, 5):
        if step > 1:
            fwd[step] = [None, None]
            bwd[step] = [None, None]
            for h in range(2):
                if step < 4 or h == 0:
                    fwd[step][h] = lax.ppermute(fwd[step - 1][h], "z", ring(NZ, 1))
                if step < 4 or h == 1:
                    bwd[step][h] = lax.ppermute(bwd[step - 1][h], "z", ring(NZ, -1))
        if step < 4:
            have[NZ - step] = fwd[step]
            have[step] = bwd[step]
        else:
            have[4] = [fwd[4][0], bwd[4][1]]

    metas[0] = hand_on(metas[0])
    got = jnp.stack([m.reshape(slots) for m in metas])
    own = got // BPD
    shift = jnp.arange(NX, dtype=jnp.int32)[:, None]
    towards = jnp.where(got < 0, NX, own % NX)
    match = towards == x
    dist = (own // NX - z) % NZ
    place = rank_in_group(towards, distance_order(dist))
    block_row = (ids // S)[None, :]
    group = jnp.where(match, 2 * dist + ((block_row % NC) ^ core), 2 * NZ)
    rank = rank_in_group(group, jnp.zeros_like(group))
    hits = (group[:, :, None] == jnp.arange(2 * NZ)[None, None, :]).astype(jnp.int32)
    counts = jnp.sum(hits, axis=1)
    offsets = jnp.cumsum(counts, axis=0) - counts
    number = jnp.sum(counts, axis=0)
    entry = jnp.sum(hits * offsets[:, None, :], axis=2) + rank
    where = jnp.where(match, group * ENTRIES + entry, -1).reshape(-1)
    row = (NX - shift) % NX * NY + (block_row // NC - y) % NY
    packed = place + 128 * shift + 512 * (got % BPD) + 16384 * row
    filling = 127
    spots = jnp.arange(2 * NZ * ENTRIES, dtype=jnp.int32)
    table = filling + jnp.sum(
        jnp.where(where[:, None] == spots[None, :], packed.reshape(-1)[:, None] - filling, 0),
        axis=0,
    )

    longest = jnp.max(jnp.where(got >= 0, place, -1)) + 1

    def second_part():
        parts = []
        for dx in range(NX):
            sent = flat_values.at[wanted[dx, FIRST:]].get(mode="promise_in_bounds")
            parts.append(lax.ppermute(sent, "x", ring(NX, dx)) if dx else sent)
        return tuple(parts)

    def no_second_part():
        return (jnp.zeros((REST, BS, BS), jnp.bfloat16),) * NX

    more = lax.cond(longest > FIRST, second_part, no_second_part)
    number = jnp.concatenate([number, longest[None]])

    prev = None
    groups = [((0, 1, 7, 2, 6), FULL), ((3, 5), 3 * CAP), ((4,), CAP)]
    for ds, window in groups:
        prev = products(ds, window, table, number, vals, more, [have[d] for d in ds], prev)
    mine, other = prev
    parts = spread(mine, lax.ppermute(other, "core", ring(NC, 1)))
    for axes in (("x", "y"), ("y", "x")):
        moved = [list(side) for side in parts]
        for r in (2, 1, 3):
            for axis, side in zip(axes, moved):
                side[r] = lax.ppermute(side[r], axis, ring(NX, r))
        if axes[0] == "x":
            parts = add_up(moved[0]), add_up(moved[1])
    gram, image_t = local_gram(*moved)
    plane = ("x", "y", "core")
    n_plane = NX * NY * NC
    piece = K // n_plane
    gram = gram.reshape(n_plane, piece, K)
    part = jnp.sum(lax.all_to_all(gram, plane, 0, 0, tiled=True), axis=0)
    part = jnp.broadcast_to(part[None], (NZ, piece, K))
    part = jnp.sum(lax.all_to_all(part, "z", 0, 0, tiled=True), axis=0) / (NZ * n_plane * BS)
    part = jnp.broadcast_to(part[None], (n_plane, piece, K))
    gram = lax.all_to_all(part, plane, 0, 0, tiled=True).reshape(K, K)
    triangle, basis = factor(gram, image_t)
    return basis, triangle


def solution(mesh):
    axes = ("z", "x", "y", "core")
    fine = Mesh(mesh.devices.reshape(NZ, NX, NY, NC), axes)
    rows, cols = ("z", "x"), ("y", "core")
    return jax.shard_map(
        one_device,
        mesh=fine,
        in_specs=(P(rows, cols, None, None), P(rows, cols), P(rows, cols), P(axes, None)),
        out_specs=(P(axes, None), P()),
        check_vma=False,
    )
```
